256 devices in a mesh: cfg: 2 (over core), req: 8 (over z), seq: 16 (over y, x).
Axes of the slice: x: 4, y: 4, z: 8, core: 2. Of those that a mesh axis runs over, the one named last changes fastest.
Arguments:
- queries: bfloat16 [2, 8, 768, 1536], P('cfg', 'req', 'seq'), may hold values from -50 to 50
- text_cache: bfloat16 [2, 8, 2, 512, 1536], P('cfg', 'req'), may hold values from -6 to 6
- image_cache: bfloat16 [2, 8, 2, 768, 1536], P('cfg', 'req'), may hold values from -6 to 6
- fresh_kv: bfloat16 [2, 8, 2, 96, 1536], P('cfg', 'req', None, 'seq'), may hold values from -6 to 6
- fresh_slots: int32 [8, 96], P('req'), may hold values from 0 to 767, as said below
- fresh_pos: int32 [3, 8, 96], P(None, 'req', 'seq'), may hold values from 0 to 63
- image_len: int32 [8], replicated, may hold values from 384 to 768, as said below
- stream: bfloat16 [2, 8, 768, 3072], P('cfg', None, 'seq', 'req'), may hold values from -30 to 30
- modulation: float32 [2, 8, 4, 3072], replicated, may hold values from -4 to 4
- out_weight: bfloat16 [1536, 3072], P('seq', 'req'), may hold values from -0.15625 to 0.15625
- up_weight: bfloat16 [3072, 12288], P('seq', 'req'), may hold values from -0.109375 to 0.109375
- down_weight: bfloat16 [12288, 3072], P('req', 'seq'), may hold values from -0.0546875 to 0.0546875
- final_weight: bfloat16 [3072, 64], replicated, may hold values from -0.109375 to 0.109375
- latent: float32 [8, 384, 128], P('req', 'seq', 'cfg'), may hold values from -6 to 6
- step_index: int32 [1], replicated, may hold values from 0 to 27
Outputs:
- latent_next: float32 [8, 384, 128], P('req', 'seq', 'cfg')
- denoised: float32 [8, 384, 128], P('req', 'seq', 'cfg')
The draws below stay inside these ranges and needn't reach their ends.
Inputs may be any that keep to these rules, and one draw needn't show every extreme that they name: `fresh_slots`: columns k * 6 to (k + 1) * 6 - 1 of a row hold distinct slots from k * 48 to (k + 1) * 48 - 1. `image_len`: some request has exactly 768 image tokens and some other exactly 384.
All inputs are finite; a program needn't handle non-finite values.
Results may differ from the reference program's by a relative error of at most 0.0095.
Values may be sent and summed in bfloat16 or wider, within the bound.
A program may use at most 128 MiB of HBM per device.

```python
import math
import jax
import jax.numpy as jnp
from jax import lax

D = 3072
LAT = 64
FFW = 12288
TXT = 512
STEPS = 28
IMG_DEV = 48
HD = 1536
R = 8
IMG_MAX = 768
FRESH_DEV = 6
FRESH = 96


def joint_attention_draw(key):
    query_key = jax.random.fold_in(key, 101)
    text_key = jax.random.fold_in(key, 102)
    query_shape = (2, R, IMG_MAX, HD)
    text_shape = (2, R, 2, TXT, HD)
    query_vals = jnp.clip(2.0 * jax.random.normal(query_key, query_shape, jnp.float32), -12.0, 12.0)
    text_vals = jnp.clip(jax.random.normal(text_key, text_shape, jnp.float32), -6.0, 6.0)
    return (query_vals.astype(jnp.bfloat16), text_vals.astype(jnp.bfloat16))


def draw_queries(key, part):
    return joint_attention_draw(key)[0]


def draw_text_cache(key, part):
    return joint_attention_draw(key)[1]


def draw_fresh_slots(key, part):
    blocks = FRESH // FRESH_DEV
    sub_keys = jax.random.split(jax.random.fold_in(key, 7), R * blocks)
    chosen = jax.vmap(lambda sub_key: jax.random.permutation(sub_key, IMG_DEV)[:FRESH_DEV])(sub_keys)
    offsets = jnp.arange(R * blocks, dtype=jnp.int32) % blocks * IMG_DEV
    return (chosen.astype(jnp.int32) + offsets[:, None]).reshape(R, FRESH)


def draw_image_len(key, part):
    lengths = jax.random.randint(jax.random.fold_in(key, 1), (R,), IMG_MAX // 2, IMG_MAX + 1)
    longest = jax.random.randint(jax.random.fold_in(key, 2), (), 0, R)
    row_ids = jnp.arange(R)
    lengths = jnp.where(row_ids == longest, IMG_MAX, lengths)
    lengths = jnp.where(row_ids == (longest + 1) % R, IMG_MAX // 2, lengths)
    return lengths.astype(jnp.int32)


def draw_stream(key, part):
    shape = (2, R, IMG_MAX, D)
    noise_key = jax.random.fold_in(key, 21)
    row_key = jax.random.fold_in(key, 22)
    col_key = jax.random.fold_in(key, 23)
    row_scale = jnp.exp(jax.random.uniform(row_key, (2, R, IMG_MAX, 1), jnp.float32, 0.0, math.log(10.0))) / 3.0
    col_scale = jnp.exp(jax.random.uniform(col_key, (1, 1, 1, D), jnp.float32, 0.0, math.log(10.0))) / 3.0
    noise = jnp.clip(jax.random.normal(noise_key, shape, jnp.float32), -5.0, 5.0)
    return jnp.clip(noise * row_scale * col_scale, -30.0, 30.0).astype(jnp.bfloat16)


def touch_ends(entries, own_key, least, top_value):
    longest = entries.shape.index(max(entries.shape))
    spots = []
    for shift in (0, 1):
        where = [jax.random.randint(jax.random.fold_in(own_key, axis), (), 0, length) for axis, length in enumerate(entries.shape)]
        where[longest] = (where[longest] + shift) % entries.shape[longest]
        spots.append(tuple(where))
    return entries.at[spots[0]].set(least).at[spots[1]].set(top_value)


def levels(key, extent, shards, low, high):
    def one(dim, shards_of):
        heights = jax.random.uniform(jax.random.fold_in(jax.random.fold_in(key, 6), dim), (shards_of,), jnp.float32, low / len(shards), high / len(shards))
        return jnp.repeat(jnp.exp(heights), extent[dim] // shards_of).reshape((-1,) + (1,) * (len(extent) - dim - 1))

    factor_of = one(*shards[0])
    for cut in shards[1:]:
        factor_of = factor_of * one(*cut)
    return factor_of


def gaussian(rng, dims, scale, bound, cuts=(), kind=jnp.bfloat16):
    factor_of = levels(rng, dims, cuts, -0.22, 0.18) if cuts else 1.0
    result = jax.random.normal(rng, dims, jnp.float32) * scale * factor_of
    return jnp.minimum(jnp.maximum(result, -bound), bound).astype(kind)


def setup_inputs(seed: int = 0) -> dict:
    splits = jax.random.split(jax.random.key(seed), 16)
    queries = draw_queries(jax.random.fold_in(splits[15], 71), 0)
    text_cache = draw_text_cache(jax.random.fold_in(splits[15], 71), 0)
    image_cache = gaussian(splits[2], (2, R, 2, IMG_MAX, HD), 1.0, 6.0, ((0, 2), (1, 8)))
    fresh_kv = gaussian(splits[3], (2, R, 2, FRESH, HD), 1.0, 6.0, ((0, 2), (1, 8), (3, 16)))
    fresh_slots = draw_fresh_slots(jax.random.fold_in(splits[15], 71), 0)
    fresh_pos = touch_ends(jax.random.randint(splits[5], (3, R, FRESH), 0, 64), jax.random.fold_in(splits[5], 1), 0, 63).astype(jnp.int32)
    image_len = draw_image_len(jax.random.fold_in(splits[15], 71), 0)
    stream = draw_stream(jax.random.fold_in(splits[15], 71), 0)
    modulation = gaussian(splits[8], (2, R, 4, D), 1.0, 4.0, (), jnp.float32)
    out_weight = gaussian(splits[9], (HD, D), HD ** -0.5, 0.15625, ((0, 16), (1, 8)))
    up_weight = gaussian(splits[10], (D, FFW), D ** -0.5, 0.109375, ((0, 16), (1, 8)))
    down_weight = gaussian(splits[11], (FFW, D), FFW ** -0.5, 0.0546875, ((0, 8), (1, 16)))
    final_weight = gaussian(splits[12], (D, LAT), D ** -0.5, 0.109375)
    latent = gaussian(splits[13], (R, IMG_MAX // 2, 2 * LAT), 1.0, 6.0, ((0, 8), (1, 16), (2, 2)), jnp.float32)
    step_index = jax.random.randint(splits[14], (1,), 0, STEPS).astype(jnp.int32)
    return {"queries": queries, "text_cache": text_cache, "image_cache": image_cache, "fresh_kv": fresh_kv, "fresh_slots": fresh_slots, "fresh_pos": fresh_pos, "image_len": image_len, "stream": stream, "modulation": modulation, "out_weight": out_weight, "up_weight": up_weight, "down_weight": down_weight, "final_weight": final_weight, "latent": latent, "step_index": step_index}


GUIDANCE = 3.0
SHIFT = 3.0
SCALE = 1.0 / math.sqrt(128.0)
EPSILON = 1e-06

def rope_angles(positions):
    columns = []
    for component, axis_span in ((0, 16), (1, 56), (2, 56)):
        pair_ids = jnp.arange(axis_span // 2, dtype=jnp.float32)
        frequency = jnp.exp(-(2.0 * pair_ids / axis_span) * math.log(10000.0))
        columns.append(positions[component].astype(jnp.float32)[:, None] * frequency[None, :])
    return jnp.concatenate(columns, axis=1)

def rotate(key_rows, angles):
    row_total = key_rows.shape[0]
    paired = key_rows.reshape(row_total, -1, 64, 2)
    cosine = jnp.cos(angles)[:, None, :]
    sine = jnp.sin(angles)[:, None, :]
    first = cosine * paired[..., 0] - sine * paired[..., 1]
    second = sine * paired[..., 0] + cosine * paired[..., 1]
    return jnp.stack([first, second], axis=-1).reshape(row_total, -1)

def noise_level(index):
    fraction = 1.0 - index.astype(jnp.float32) / STEPS
    return SHIFT * fraction / (SHIFT * fraction + 1.0 - fraction)

def attend(query_rows, text_kv, image_kv, length):
    query_count = query_rows.shape[0]
    query_heads = query_rows.astype(jnp.float32).reshape(query_count, -1, 128)
    key_rows = jnp.concatenate([text_kv[0], image_kv[0]], axis=0).astype(jnp.float32)
    value_rows = jnp.concatenate([text_kv[1], image_kv[1]], axis=0).astype(jnp.float32)
    key_heads = key_rows.reshape(key_rows.shape[0], -1, 128)
    value_heads = value_rows.reshape(value_rows.shape[0], -1, 128)
    scores = jnp.einsum('qhd,khd->hqk', query_heads, key_heads) * SCALE
    key_place = jnp.concatenate([jnp.zeros((TXT,), jnp.int32), jnp.arange(IMG_MAX, dtype=jnp.int32)])
    scores = jnp.where((key_place < length)[None, None, :], scores, -jnp.inf)
    row_max = lax.optimization_barrier(jnp.max(scores, axis=-1, keepdims=True))
    probs = jnp.exp(scores - row_max)
    total = lax.optimization_barrier(jnp.sum(probs, axis=-1))
    weights = lax.optimization_barrier(probs.astype(jnp.bfloat16)).astype(jnp.float32)
    mixed = jnp.einsum('hqk,khd->qhd', weights, value_heads) / jnp.transpose(total)[:, :, None]
    return mixed.reshape(query_count, -1).astype(jnp.bfloat16)

def reference(queries, text_cache, image_cache, fresh_kv, fresh_slots, fresh_pos, image_len, stream, modulation, out_weight, up_weight, down_weight, final_weight, latent, step_index):
    angles = rope_angles(fresh_pos.reshape(3, R * FRESH))
    angles = jnp.tile(angles, (2, 1))
    fresh_keys = rotate(fresh_kv[:, :, 0].astype(jnp.float32).reshape(2 * R * FRESH, HD), angles)
    fresh_keys = fresh_keys.astype(jnp.bfloat16).reshape(2, R, FRESH, HD)
    fresh_pair = jnp.stack([fresh_keys, fresh_kv[:, :, 1]], axis=2)
    slot_table = jnp.tile(fresh_slots, (2, 1)).astype(jnp.int32)
    lengths = jnp.tile(image_len, 2)

    def one_request(items):
        query_rows, text_kv, image_kv, pair_rows, slot_ids, length = items
        image_kv = image_kv.at[:, slot_ids, :].set(pair_rows)
        return attend(query_rows, text_kv, image_kv, length)
    attended = lax.map(one_request, (queries.reshape(2 * R, IMG_MAX, HD), text_cache.reshape(2 * R, 2, TXT, HD), image_cache.reshape(2 * R, 2, IMG_MAX, HD), fresh_pair.reshape(2 * R, 2, FRESH, HD), slot_table, lengths))

    def layer(items):
        attended_rows, stream_rows, mod_rows = items
        projected = jnp.dot(attended_rows, out_weight, preferred_element_type=jnp.float32)
        residual = (stream_rows.astype(jnp.float32) + mod_rows[0][None, :] * projected).astype(jnp.bfloat16)
        wide = residual.astype(jnp.float32)
        average = lax.optimization_barrier(jnp.mean(wide, axis=-1, keepdims=True))
        centered = wide - average
        spread = lax.optimization_barrier(jnp.mean(centered * centered, axis=-1, keepdims=True))
        normed = (centered * lax.rsqrt(spread + EPSILON) * (1.0 + mod_rows[2][None, :]) + mod_rows[1][None, :]).astype(jnp.bfloat16)
        activated = jax.nn.gelu(jnp.dot(normed, up_weight, preferred_element_type=jnp.float32), approximate=True).astype(jnp.bfloat16)
        mlp_out = jnp.dot(activated, down_weight, preferred_element_type=jnp.float32)
        block_out = (wide + mod_rows[3][None, :] * mlp_out).astype(jnp.bfloat16)
        return jnp.dot(block_out, final_weight, preferred_element_type=jnp.float32)
    velocity = lax.map(layer, (attended, stream.reshape(2 * R, IMG_MAX, D), modulation.reshape(2 * R, 4, D)))
    velocity = velocity.reshape(2, R, IMG_MAX // 2, 2 * LAT)
    guided = velocity[1] + GUIDANCE * (velocity[0] - velocity[1])
    level_now = noise_level(step_index[0])
    level_next = noise_level(step_index[0] + 1)
    token_ids = 2 * jnp.arange(IMG_MAX // 2, dtype=jnp.int32)[:, None] + jnp.arange(2 * LAT, dtype=jnp.int32)[None, :] // LAT
    valid = token_ids[None, :, :] < image_len[:, None, None]
    latent_next = jnp.where(valid, latent + (level_next - level_now) * guided, latent)
    denoised = jnp.where(valid, latent - level_now * guided, latent)
    return (latent_next, denoised)
```

```python
import functools
import math

import jax
import jax.numpy as jnp
from jax import lax
from jax.experimental import pallas as pl
from jax.experimental.pallas import tpu as pltpu
from jax.sharding import PartitionSpec as P

STEPS = 28
GUIDANCE = 3.0
SHIFT = 3.0
SCALE = 1.0 / math.sqrt(128.0)
EPSILON = 1e-06
MESH = pl.DeviceIdType.MESH
F32 = jnp.float32
BF16 = jnp.bfloat16
NEG = -jnp.inf

ITEMS = ("fresh", "out", "up", "down")
OPS = ("1R", "1L", "1RR", "1LL", "2R", "2L", "2RR", "2LL", "Xa", "Xb", "Xc", "Ya", "Yb", "Yc")
N_PLANE = len(ITEMS) * len(OPS)
RING_OPS = ("R1", "R2", "R3", "R4", "L1", "L2", "L3", "L4")
N_RING = 2 * len(RING_OPS)
N_VEL = 8
N_COPY = N_PLANE + N_RING + N_VEL + 1


def nt_dot(a, b):
    return lax.dot_general(a, b, (((1,), (1,)), ((), ())), preferred_element_type=F32)


def kernel(
    len_ref,
    lev_ref,
    q_hbm,
    text_hbm,
    img_hbm,
    fresh_ref,
    cs_ref,
    srow_ref,
    scol_ref,
    stream_ref,
    mod_hbm,
    out_hbm,
    up_hbm,
    down_hbm,
    wf_ref,
    lat_ref,
    next_ref,
    den_ref,
    q_ref,
    text,
    img,
    mod,
    fbuf,
    obuf,
    ubuf,
    dbuf,
    abuf,
    rbuf,
    nbuf,
    actbuf,
    att_o,
    att_m,
    att_l,
    vel,
    velin,
    vsum,
    vother,
    load_sem,
    send_sem,
    recv_sem,
):
    c = lax.axis_index("cfg")
    z = lax.axis_index("req")
    s = lax.axis_index("seq")
    y = s // 4
    x = s % 4

    def ring8(i):
        return lax.rem(z + i + 8, 8)

    started = []

    loads = {}

    def load(name, src, dst):
        loads[name] = pltpu.make_async_copy(src, dst, load_sem.at[len(loads)])
        loads[name].start()

    load("q", q_hbm, q_ref)
    load("tk", text_hbm.at[0], text.at[0])
    load("ik", img_hbm.at[0], img.at[0])
    load("tv", text_hbm.at[1], text.at[1])
    load("iv", img_hbm.at[1], img.at[1])
    load("o", out_hbm, obuf.at[y, x])
    load("u", up_hbm, ubuf.at[y, x])
    load("d", down_hbm, dbuf.at[y, x])
    load("mod", mod_hbm.at[c], mod)

    bufs = {"fresh": fbuf, "out": obuf, "up": ubuf, "down": dbuf}
    shards = {"out": out_hbm, "up": up_hbm, "down": down_hbm}

    def plane(item, op, core):
        buf = bufs[item]
        u, v = (x, y) if core == 0 else (y, x)
        own = () if item == "fresh" else (core,)

        def mod4(i):
            return lax.rem(i + 4, 4)

        def at(uu, vv, extra=()):
            where = (vv, uu) if core == 0 else (uu, vv)
            return buf.at[where + own + extra]

        def device(uu, vv):
            return {"seq": vv * 4 + uu if core == 0 else uu * 4 + vv}

        if item == "fresh":
            halves = ((slice(None), pl.ds(0, 768)), (slice(None), pl.ds(768, 768)))
        elif item == "out":
            halves = ((pl.ds(0, 32),), (pl.ds(32, 16),))
        else:
            halves = ((pl.ds(0, 48),), (pl.ds(48, 48),))
        right1, left1 = device(mod4(u + 1), v), device(mod4(u - 1), v)
        right2, left2 = device(u, mod4(v + 1)), device(u, mod4(v - 1))
        partner = {"cfg": 1 - core}
        every = slice(None)
        if op in ("1R", "1L"):
            dst = at(u, v)
            src = dst if item == "fresh" else shards[item].at[core]
            dev = right1 if op == "1R" else left1
        elif op == "1RR":
            src = dst = at(mod4(u - 1), v, halves[0])
            dev = right1
        elif op == "1LL":
            src = dst = at(mod4(u + 1), v, halves[1])
            dev = left1
        elif op in ("2R", "2L"):
            src = dst = at(every, v)
            dev = right2 if op == "2R" else left2
        elif op == "2RR":
            src = dst = at(pl.ds(0, 2), mod4(v - 1))
            dev = right2
        elif op == "2LL":
            src = dst = at(pl.ds(2, 2), mod4(v + 1))
            dev = left2
        else:
            step = {"a": -1, "b": 1, "c": 2}[op[1]]
            src = dst = at(mod4(u + step), v) if op[0] == "X" else at(every, mod4(v + step))
            dev = partner
        index = ITEMS.index(item) * len(OPS) + OPS.index(op)
        return pltpu.make_async_remote_copy(
            src_ref=src,
            dst_ref=dst,
            send_sem=send_sem.at[index],
            recv_sem=recv_sem.at[index],
            device_id=dev,
            device_id_type=MESH,
        )

    def arrival(item, op, core):
        buf = bufs[item]
        u, v = (x, y) if core == 0 else (y, x)
        return plane(item, op, core)

    plane_log = []

    def both(act):
        for core in (0, 1):
            pl.when(c == core)(functools.partial(act, core))

    def go(item, *ops):
        for op in ops:
            plane_log.append((item, op))

        def act(core):
            for op in ops:
                plane(item, op, core).start()

        both(act)

    def serve(item, steps):
        for _, after in steps:
            for op in after:
                plane_log.append((item, op))

        def act(core):
            for op, after in steps:
                plane(item, op, core).wait_recv()
                for follow in after:
                    plane(item, follow, core).start()

        both(act)

    def take(item, ops):
        def act(core):
            for op in ops:
                plane(item, op, 1 - core).wait_recv()

        both(act)

    def ring(which, op):
        buf = (abuf, rbuf)[which]
        k = int(op[1])
        right = op[0] == "R"
        owner = ring8(1 - k if right else k - 1)
        if k < 4:
            src = buf.at[owner]
        elif which == 0:
            src = buf.at[owner, :, pl.ds(0 if right else 768, 768)]
        else:
            src = buf.at[owner, pl.ds(0 if right else 4, 4)]
        index = N_PLANE + which * len(RING_OPS) + RING_OPS.index(op)
        return pltpu.make_async_remote_copy(
            src_ref=src,
            dst_ref=src,
            send_sem=send_sem.at[index],
            recv_sem=recv_sem.at[index],
            device_id={"req": ring8(1 if right else -1)},
            device_id_type=MESH,
        )

    def ring_go(which, *ops):
        for op in ops:
            ring(which, op).start()
            started.append(ring(which, op))

    lane = lax.broadcasted_iota(jnp.int32, (8, 128), 1)
    even = lax.rem(lane, 2) == 0
    cosine = cs_ref[0]
    sine = cs_ref[1]
    for h in range(12):
        k = fresh_ref[0, :, h * 128 : (h + 1) * 128].astype(F32)
        swapped = jnp.where(even, pltpu.roll(k, 127, 1), pltpu.roll(k, 1, 1))
        turned = k * cosine + swapped * sine
        v = fresh_ref[1, :, h * 128 : (h + 1) * 128].astype(F32)
        fbuf[y, x, :, h * 128 : (h + 1) * 128] = jnp.concatenate([turned, v], axis=0).astype(BF16)

    barrier = pltpu.get_barrier_semaphore()
    greeted = [{"cfg": 1 - c}]
    for step in (1, 3):
        greeted.append({"seq": y * 4 + lax.rem(x + step, 4)})
        greeted.append({"seq": lax.rem(y + step, 4) * 4 + x})
    for step in range(1, 8):
        greeted.append({"req": ring8(step)})
    for device in greeted:
        pl.semaphore_signal(barrier, inc=1, device_id=device, device_id_type=MESH)
    pl.semaphore_wait(barrier, len(greeted))

    go("fresh", "1R", "1L")

    length = len_ref[z]
    slot_hit = jnp.max(
        (scol_ref[...] == lax.broadcasted_iota(jnp.int32, (128, 768), 1)).astype(F32),
        axis=0,
        keepdims=True,
    )
    key_place = lax.broadcasted_iota(jnp.int32, (1, 768), 1)
    bias_img = jnp.where((key_place < length) & (slot_hit < 0.5), 0.0, NEG).astype(F32)
    slot_row = srow_ref[...]
    bias_new = jnp.where((slot_row >= 0) & (slot_row < length), 0.0, NEG).astype(F32)
    bias_new = jnp.broadcast_to(bias_new[0:1], (1, 128))

    def cached_heads(first, count):
        def one(h, carry):
            cols = pl.ds(pl.multiple_of(h * 128, 128), 128)
            q = q_ref[:, cols]
            st = nt_dot(q, text[0, :, cols]) * SCALE
            si = nt_dot(q, img[0, :, cols]) * SCALE + bias_img
            m = jnp.maximum(
                jnp.max(st, axis=-1, keepdims=True), jnp.max(si, axis=-1, keepdims=True)
            )
            pt = jnp.exp(st - m)
            pi = jnp.exp(si - m)
            total = jnp.sum(pt, axis=-1, keepdims=True) + jnp.sum(pi, axis=-1, keepdims=True)
            o = jnp.dot(pt.astype(BF16), text[1, :, cols], preferred_element_type=F32)
            o = o + jnp.dot(pi.astype(BF16), img[1, :, cols], preferred_element_type=F32)
            att_o[h] = o
            att_m[h] = jnp.broadcast_to(m, (48, 128))
            att_l[h] = jnp.broadcast_to(total, (48, 128))
            return carry

        lax.fori_loop(first, first + count, one, 0)

    for name in ("q", "tk", "ik", "tv", "iv"):
        loads[name].wait()
    cached_heads(0, 3)
    serve("fresh", [("1R", ["1RR"]), ("1L", ["1LL"])])
    go("out", "1R", "1L")
    go("up", "1R", "1L")
    cached_heads(3, 3)
    serve("fresh", [("1RR", []), ("1LL", ["2R", "2L"])])
    cached_heads(6, 3)
    serve("out", [("1R", ["1RR", "Xa"]), ("1L", ["1LL", "Xb"])])
    serve("fresh", [("2R", ["2RR"]), ("2L", ["2LL"])])
    go("down", "1R", "1L")
    cached_heads(9, 3)
    loads["o"].wait()
    serve("out", [("1RR", []), ("1LL", ["2R", "2L", "Xc"])])
    serve("fresh", [("2RR", []), ("2LL", [])])

    def fresh_head(h, carry):
        cols = pl.ds(pl.multiple_of(h * 128, 128), 128)
        q = q_ref[:, cols]
        kv = fbuf[:, :, :, cols].astype(F32)
        kf = kv[:, :, :8].reshape(128, 128).astype(BF16)
        vf = kv[:, :, 8:].reshape(128, 128).astype(BF16)
        sf = nt_dot(q, kf) * SCALE + bias_new
        before = att_m[h][:, 0:1]
        m = jnp.maximum(before, jnp.max(sf, axis=-1, keepdims=True))
        pf = jnp.exp(sf - m)
        keep = jnp.exp(before - m)
        total = att_l[h][:, 0:1] * keep + jnp.sum(pf, axis=-1, keepdims=True)
        o = att_o[h] * keep + jnp.dot(pf.astype(BF16), vf, preferred_element_type=F32)
        abuf[z, :, cols] = (o / total).astype(BF16)
        return carry

    lax.fori_loop(0, 12, fresh_head, 0)

    def project(r):
        rows = jnp.dot(abuf[r], obuf[...].reshape(1536, 384), preferred_element_type=F32)
        gate = mod[r, 0:1, pl.ds(pl.multiple_of(z * 384, 128), 384)]
        rbuf[z, r] = (stream_ref[r].astype(F32) + gate * rows).astype(BF16)

    ring_go(0, "R1", "L1")
    serve("out", [("2R", ["2RR", "Ya"]), ("2L", ["2LL", "Yb"])])
    serve("up", [("1R", ["1RR", "Xa"]), ("1L", ["1LL", "Xb"])])
    ring(0, "R1").wait_recv()
    ring_go(0, "R2")
    ring(0, "L1").wait_recv()
    ring_go(0, "L2")
    serve("out", [("2RR", []), ("2LL", ["Yc"])])
    loads["u"].wait()
    serve("up", [("1RR", []), ("1LL", ["2R", "2L", "Xc"])])
    take("out", ("Xa", "Xb", "Xc", "Ya", "Yb", "Yc"))
    loads["mod"].wait()
    project(z)
    ring(0, "R2").wait_recv()
    ring_go(0, "R3")
    ring(0, "L2").wait_recv()
    ring_go(0, "L3")
    serve("down", [("1R", ["1RR", "Xa"]), ("1L", ["1LL", "Xb"])])
    project(ring8(-1))
    project(ring8(1))
    ring(0, "R3").wait_recv()
    ring_go(0, "R4")
    ring(0, "L3").wait_recv()
    ring_go(0, "L4")
    loads["d"].wait()
    serve("down", [("1RR", []), ("1LL", ["2R", "2L", "Xc"])])
    project(ring8(-2))
    project(ring8(2))
    project(ring8(-3))
    project(ring8(3))
    ring(0, "R4").wait_recv()
    ring(0, "L4").wait_recv()
    project(ring8(4))

    ring_go(1, "R1", "L1")
    serve("up", [("2R", ["2RR", "Ya"]), ("2L", ["2LL", "Yb"])])
    ring(1, "R1").wait_recv()
    ring_go(1, "R2")
    ring(1, "L1").wait_recv()
    ring_go(1, "L2")
    ring(1, "R2").wait_recv()
    ring_go(1, "R3")
    ring(1, "L2").wait_recv()
    ring_go(1, "L3")
    serve("up", [("2RR", []), ("2LL", ["Yc"])])
    ring(1, "R3").wait_recv()
    ring_go(1, "R4")
    ring(1, "L3").wait_recv()
    ring_go(1, "L4")
    ring(1, "R4").wait_recv()
    ring(1, "L4").wait_recv()
    serve("down", [("2R", ["2RR", "Ya"]), ("2L", ["2LL", "Yb"])])

    def normalize(r, carry):
        parts = [rbuf[b, r].astype(F32) for b in range(8)]
        row_sum = sum(jnp.sum(p, axis=-1, keepdims=True) for p in parts)
        average = row_sum * (1.0 / 3072.0)
        centered = [p - average for p in parts]
        spread = sum(jnp.sum(p * p, axis=-1, keepdims=True) for p in centered) * (1.0 / 3072.0)
        inverse = lax.rsqrt(spread + EPSILON)
        for b in range(8):
            cols = pl.ds(b * 384, 384)
            gain = 1.0 + mod[r, 2:3, cols]
            shift = mod[r, 1:2, cols]
            nbuf[r, :, cols] = (centered[b] * inverse * gain + shift).astype(BF16)
        return carry

    lax.fori_loop(0, 8, normalize, 0)

    take("up", ("Xa", "Xb", "Xc", "Ya", "Yb", "Yc"))

    def up_tile(t, carry):
        cols = pl.ds(pl.multiple_of(t * 256, 256), 256)
        pre = jnp.dot(
            nbuf[...].reshape(384, 3072),
            ubuf[:, :, :, :, cols].reshape(3072, 256),
            preferred_element_type=F32,
        )
        actbuf[:, cols] = jax.nn.gelu(pre, approximate=True).astype(BF16)
        return carry

    lax.fori_loop(0, 6, up_tile, 0)
    serve("down", [("2RR", []), ("2LL", ["Yc"])])
    take("down", ("Xa", "Xb", "Xc", "Ya", "Yb", "Yc"))

    vel[...] = jnp.zeros_like(vel)

    def down_tile(t, carry):
        cols = pl.ds(pl.multiple_of(t * 768, 256), 768)
        mlp = nt_dot(actbuf[...], dbuf[t].reshape(768, 1536)).reshape(8, 48, 768)
        gated = (mlp * mod[:, 3:4, cols]).astype(BF16).reshape(384, 768)
        vel[:, :, 0:64] += nt_dot(gated, wf_ref[:, cols]).reshape(8, 48, 64)
        return carry

    lax.fori_loop(0, 4, down_tile, 0)

    def velocity_copy(step):
        target = ring8(step)
        index = N_PLANE + N_RING + step
        return pltpu.make_async_remote_copy(
            src_ref=vel.at[target],
            dst_ref=velin.at[step],
            send_sem=send_sem.at[index],
            recv_sem=recv_sem.at[index],
            device_id={"req": target},
            device_id_type=MESH,
        )

    for step in range(1, 8):
        velocity_copy(step).start()
        started.append(velocity_copy(step))
    own = jnp.concatenate([rbuf[b, z] for b in range(8)], axis=-1)
    total = vel[z][:, 0:64] + nt_dot(own, wf_ref[...])
    for step in range(1, 8):
        velocity_copy(step).wait_recv()
        total = total + velin[step][:, 0:64]
    vsum[:, 0:64] = total
    vsum[:, 64:128] = total
    swap = pltpu.make_async_remote_copy(
        src_ref=vsum,
        dst_ref=vother,
        send_sem=send_sem.at[N_COPY - 1],
        recv_sem=recv_sem.at[N_COPY - 1],
        device_id={"cfg": 1 - c},
        device_id_type=MESH,
    )
    swap.start()
    started.append(swap)
    swap.wait_recv()

    first = c == 0
    mine = jnp.where(first, vsum[pl.ds(0, 24, stride=2), :], vsum[pl.ds(1, 24, stride=2), :])
    theirs = jnp.where(first, vother[pl.ds(0, 24, stride=2), :], vother[pl.ds(1, 24, stride=2), :])
    cond = jnp.where(first, mine, theirs)[:, 0:64]
    uncond = jnp.where(first, theirs, mine)[:, 0:64]
    guided = uncond + GUIDANCE * (cond - uncond)
    token = s * 48 + 2 * lax.broadcasted_iota(jnp.int32, (24, 64), 0) + c
    valid = token < length
    current = lat_ref[...]
    now = lev_ref[0]
    later = lev_ref[1]
    next_ref[...] = jnp.where(valid, current + (later - now) * guided, current)
    den_ref[...] = jnp.where(valid, current - now * guided, current)

    def finish(core):
        for item, op in plane_log:
            plane(item, op, core).wait_send()

    both(finish)
    for copy in started:
        copy.wait_send()


def rope_tables(positions):
    lane = jnp.arange(128, dtype=jnp.int32)
    pair = lane // 2
    offset = jnp.where(pair < 8, 0, jnp.where(pair < 36, 8, 36))
    span = jnp.where(pair < 8, 16.0, 56.0).astype(F32)
    frequency = jnp.exp(-(2.0 * (pair - offset).astype(F32) / span) * math.log(10000.0))
    place = positions.astype(F32)[:, :, None]
    chosen = jnp.where(pair < 8, place[0], jnp.where(pair < 36, place[1], place[2]))
    angle = chosen * frequency
    sine = jnp.sin(angle)
    return jnp.stack([jnp.cos(angle), jnp.where(lane % 2 == 0, -sine, sine)])


def noise_level(index):
    fraction = 1.0 - index.astype(F32) / STEPS
    return SHIFT * fraction / (SHIFT * fraction + 1.0 - fraction)


def per_device(
    queries,
    text_cache,
    image_cache,
    fresh_kv,
    fresh_slots,
    fresh_pos,
    image_len,
    stream,
    modulation,
    out_weight,
    up_weight,
    down_weight,
    final_weight,
    latent,
    step_index,
):
    fresh = jnp.pad(fresh_kv[0, 0], ((0, 0), (0, 2), (0, 0)))
    tables = rope_tables(jnp.pad(fresh_pos[:, 0, :], ((0, 0), (0, 2))))
    slots = jnp.pad(fresh_slots.reshape(16, 6), ((0, 0), (0, 2)), constant_values=-1)
    index = step_index[0] + jnp.arange(2, dtype=jnp.int32)
    levels = noise_level(index)
    vmem = pl.BlockSpec(memory_space=pltpu.VMEM)
    smem = pl.BlockSpec(memory_space=pltpu.SMEM)
    hbm = pl.BlockSpec(memory_space=pl.ANY)
    out = jax.ShapeDtypeStruct((24, 64), F32)
    latent_next, denoised = pl.pallas_call(
        kernel,
        out_shape=(out, out),
        in_specs=[smem, smem, hbm, hbm, hbm, vmem, vmem, vmem, vmem, vmem, hbm, hbm, hbm, hbm, vmem, vmem],
        out_specs=(vmem, vmem),
        scratch_shapes=[
            pltpu.VMEM((48, 1536), BF16),
            pltpu.VMEM((2, 512, 1536), BF16),
            pltpu.VMEM((2, 768, 1536), BF16),
            pltpu.VMEM((8, 4, 3072), F32),
            pltpu.VMEM((4, 4, 16, 1536), BF16),
            pltpu.VMEM((4, 4, 2, 48, 384), BF16),
            pltpu.VMEM((4, 4, 2, 96, 1536), BF16),
            pltpu.VMEM((4, 4, 2, 96, 1536), BF16),
            pltpu.VMEM((8, 48, 1536), BF16),
            pltpu.VMEM((8, 8, 48, 384), BF16),
            pltpu.VMEM((8, 48, 3072), BF16),
            pltpu.VMEM((384, 1536), BF16),
            pltpu.VMEM((12, 48, 128), F32),
            pltpu.VMEM((12, 48, 128), F32),
            pltpu.VMEM((12, 48, 128), F32),
            pltpu.VMEM((8, 48, 128), F32),
            pltpu.VMEM((8, 48, 128), F32),
            pltpu.VMEM((48, 128), F32),
            pltpu.VMEM((48, 128), F32),
            pltpu.SemaphoreType.DMA((9,)),
            pltpu.SemaphoreType.DMA((N_COPY,)),
            pltpu.SemaphoreType.DMA((N_COPY,)),
        ],
        compiler_params=pltpu.CompilerParams(
            collective_id=0, has_side_effects=True, vmem_limit_bytes=60 * 1024 * 1024
        ),
    )(
        image_len,
        levels,
        queries[0, 0],
        text_cache[0, 0],
        image_cache[0, 0],
        fresh,
        tables,
        slots.reshape(1, 128),
        slots.reshape(128, 1),
        stream[0],
        modulation,
        out_weight.reshape(2, 48, 384),
        up_weight.reshape(2, 96, 1536),
        down_weight.T.reshape(2, 96, 1536),
        final_weight.T,
        latent[0],
    )
    return (latent_next[None], denoised[None])


def solution(mesh):
    in_specs = (
        P("cfg", "req", "seq", None),
        P("cfg", "req", None, None, None),
        P("cfg", "req", None, None, None),
        P("cfg", "req", None, "seq", None),
        P("req", None),
        P(None, "req", "seq"),
        P(),
        P("cfg", None, "seq", "req"),
        P(),
        P("seq", "req"),
        P("seq", "req"),
        P("req", "seq"),
        P(),
        P("req", "seq", "cfg"),
        P(),
    )
    out_specs = (P("req", "seq", "cfg"), P("req", "seq", "cfg"))
    return jax.shard_map(
        per_device, mesh=mesh, in_specs=in_specs, out_specs=out_specs, check_vma=False
    )
```

```python
import functools
import math

import jax
import jax.numpy as jnp
from jax import lax
from jax.experimental import pallas as pl
from jax.experimental.pallas import tpu as pltpu
from jax.sharding import PartitionSpec as P

STEPS = 28
GUIDANCE = 3.0
SHIFT = 3.0
SCALE = 1.0 / math.sqrt(128.0)
EPSILON = 1e-06
MESH = pl.DeviceIdType.MESH
F32 = jnp.float32
BF16 = jnp.bfloat16
NEG = -jnp.inf
SKIP = frozenset()

ITEMS = ("fresh", "out", "up0", "up1", "down0", "down1")
OPS = ("1R", "1L", "1RR", "1LL", "2R", "2L", "2RR", "2LL", "Xa", "Xb", "Xc", "Ya", "Yb", "Yc")
N_PLANE = len(ITEMS) * len(OPS)
RING_OPS = ("R1", "R2", "R3", "R4", "L1", "L2", "L3", "L4")
N_RING = 4 * len(RING_OPS)
N_VEL = 8
N_COPY = N_PLANE + N_RING + N_VEL + 1


def nt_dot(a, b):
    return lax.dot_general(a, b, (((1,), (1,)), ((), ())), preferred_element_type=F32)


def nn_dot(a, b):
    return jnp.dot(a, b, preferred_element_type=F32)


def noise_level(index):
    fraction = 1.0 - index.astype(F32) / STEPS
    return SHIFT * fraction / (SHIFT * fraction + 1.0 - fraction)


def kernel(
    len_ref,
    step_ref,
    slot_ref,
    pos_ref,
    q_hbm,
    text_hbm,
    img_hbm,
    fresh_ref,
    stream_hbm,
    mod_hbm,
    out_hbm,
    up_hbm,
    down_hbm,
    wf_hbm,
    lat_ref,
    res_ref,
    q_ref,
    text,
    img,
    stream,
    mod,
    wf,
    ftmp,
    fbuf,
    obuf,
    ubuf,
    dbuf,
    abuf,
    rbuf,
    nbuf,
    actbuf,
    mlp,
    att_o,
    att_m,
    att_l,
    vel,
    swap_out,
    swap_in,
    part,
    partin,
    load_sem,
    send_sem,
    recv_sem,
):
    c = lax.axis_index("cfg")
    z = lax.axis_index("req")
    s = lax.axis_index("seq")
    y = s // 4
    x = s % 4

    def ring8(i):
        return lax.rem(z + i + 8, 8)

    started = []

    loads = {}

    def load(name, src, dst):
        loads[name] = pltpu.make_async_copy(src, dst, load_sem.at[len(loads)])
        loads[name].start()

    load("q", q_hbm, q_ref)
    load("tk", text_hbm.at[0], text.at[0])
    load("ik", img_hbm.at[0], img.at[0])
    load("tv", text_hbm.at[1], text.at[1])
    load("iv", img_hbm.at[1], img.at[1])
    load("out", out_hbm, obuf.at[y, x])
    for half in (0, 1):
        load("up%d" % half, up_hbm.at[:, :, pl.ds(768 * half, 768)], ubuf.at[half, y, x])
    for half in (0, 1):
        load("down%d" % half, down_hbm.at[:, :, pl.ds(768 * half, 768)], dbuf.at[half, y, x])
    load("stream", stream_hbm, stream)
    load("mod", mod_hbm.at[c], mod)
    load("wf", wf_hbm, wf)

    def plane(item, op, core):
        half = int(item[-1]) if item[-1] in "01" else 0
        if item == "fresh":
            buf, shard = fbuf, None
        elif item == "out":
            buf, shard = obuf, out_hbm.at[core]
        elif item[:2] == "up":
            buf, shard = ubuf.at[half], up_hbm.at[core, :, pl.ds(768 * half, 768)]
        else:
            buf, shard = dbuf.at[half], down_hbm.at[core, :, pl.ds(768 * half, 768)]
        u, v = (x, y) if core == 0 else (y, x)
        own = () if item == "fresh" else (core,)

        def mod4(i):
            return lax.rem(i + 4, 4)

        def at(uu, vv, extra=()):
            where = (vv, uu) if core == 0 else (uu, vv)
            return buf.at[where + own + extra]

        def device(uu, vv):
            return {"seq": vv * 4 + uu if core == 0 else uu * 4 + vv}

        if item == "fresh":
            halves = ((slice(None), pl.ds(0, 768)), (slice(None), pl.ds(768, 768)))
        elif item == "out":
            halves = ((pl.ds(0, 32),), (pl.ds(32, 16),))
        else:
            halves = ((pl.ds(0, 48),), (pl.ds(48, 48),))
        right1, left1 = device(mod4(u + 1), v), device(mod4(u - 1), v)
        right2, left2 = device(u, mod4(v + 1)), device(u, mod4(v - 1))
        every = slice(None)
        if op in ("1R", "1L"):
            dst = at(u, v)
            src = dst if item == "fresh" else shard
            dev = right1 if op == "1R" else left1
        elif op == "1RR":
            src = dst = at(mod4(u - 1), v, halves[0])
            dev = right1
        elif op == "1LL":
            src = dst = at(mod4(u + 1), v, halves[1])
            dev = left1
        elif op in ("2R", "2L"):
            src = dst = at(every, v)
            dev = right2 if op == "2R" else left2
        elif op == "2RR":
            src = dst = at(pl.ds(0, 2), mod4(v - 1))
            dev = right2
        elif op == "2LL":
            src = dst = at(pl.ds(2, 2), mod4(v + 1))
            dev = left2
        else:
            step = {"a": -1, "b": 1, "c": 2}[op[1]]
            src = dst = at(mod4(u + step), v) if op[0] == "X" else at(every, mod4(v + step))
            dev = {"cfg": 1 - core}
        index = ITEMS.index(item) * len(OPS) + OPS.index(op)
        return pltpu.make_async_remote_copy(
            src_ref=src,
            dst_ref=dst,
            send_sem=send_sem.at[index],
            recv_sem=recv_sem.at[index],
            device_id=dev,
            device_id_type=MESH,
        )

    plane_log = []

    def both(act):
        for core in (0, 1):
            pl.when(c == core)(functools.partial(act, core))

    def serve(*steps):
        steps = [step for step in steps if step[0] not in SKIP]
        for item, _, after in steps:
            plane_log.extend((item, op) for op in after.split())

        def act(core):
            for item, op, after in steps:
                if op:
                    plane(item, op, core).wait_recv()
                for follow in after.split():
                    plane(item, follow, core).start()

        if steps:
            both(act)

    def first(item):
        serve((item, None, "1R 1L"))

    def second(item):
        hand = item != "fresh"
        serve((item, "1R", "1RR Xa" if hand else "1RR"), (item, "1L", "1LL Xb" if hand else "1LL"))

    def third(item):
        if item in loads:
            loads[item].wait()
        hand = item != "fresh"
        serve((item, "1RR", ""), (item, "1LL", "2R 2L Xc" if hand else "2R 2L"))

    def fourth(item):
        hand = item != "fresh"
        serve((item, "2R", "2RR Ya" if hand else "2RR"), (item, "2L", "2LL Yb" if hand else "2LL"))

    def fifth(item):
        hand = item != "fresh"
        serve((item, "2RR", ""), (item, "2LL", "Yc" if hand else ""))

    def take(item):
        if item in SKIP:
            return

        def act(core):
            for op in ("Xa", "Xb", "Xc", "Ya", "Yb", "Yc"):
                plane(item, op, 1 - core).wait_recv()

        both(act)

    def ring(which, chunk, op):
        k = int(op[1])
        right = op[0] == "R"
        owner = ring8(1 - k if right else k - 1)
        if which == 0:
            src = abuf.at[owner, :, pl.ds(768 * chunk, 768)]
        else:
            src = rbuf.at[owner, pl.ds(4 * chunk, 4)]
        index = N_PLANE + (which * 2 + chunk) * len(RING_OPS) + RING_OPS.index(op)
        return pltpu.make_async_remote_copy(
            src_ref=src,
            dst_ref=src,
            send_sem=send_sem.at[index],
            recv_sem=recv_sem.at[index],
            device_id={"req": ring8(1 if right else -1)},
            device_id_type=MESH,
        )

    def ring_go(which, chunk, *ops):
        for op in ops:
            if "ring%d" % which not in SKIP:
                ring(which, chunk, op).start()
                started.append(ring(which, chunk, op))

    def hop(which, chunk, k):
        if "ring%d" % which in SKIP:
            return
        for side in "RL":
            if k < 4 or chunk == "RL".index(side):
                ring(which, chunk, side + str(k)).wait_recv()
            if k < 3 or (k == 3 and chunk == "RL".index(side)):
                ring_go(which, chunk, side + str(k + 1))

    barrier = pltpu.get_barrier_semaphore()
    greeted = [{"cfg": 1 - c}]
    for step in (1, 3):
        greeted.append({"seq": y * 4 + lax.rem(x + step, 4)})
        greeted.append({"seq": lax.rem(y + step, 4) * 4 + x})
    for step in range(1, 8):
        greeted.append({"req": ring8(step)})
    for device in greeted:
        pl.semaphore_signal(barrier, inc=1, device_id=device, device_id_type=MESH)

    lane = lax.broadcasted_iota(jnp.int32, (8, 128), 1)
    row = lax.broadcasted_iota(jnp.int32, (8, 128), 0)
    pair = lane // 2
    offset = jnp.where(pair < 8, 0, jnp.where(pair < 36, 8, 36))
    span = jnp.where(pair < 8, 16.0, 56.0)
    frequency = jnp.exp(-(2.0 * (pair - offset).astype(F32) / span) * math.log(10000.0))
    place = jnp.zeros((8, 128), F32)
    for j in range(6):
        ids = [jnp.full((8, 128), pos_ref[axis, 0, j], jnp.int32).astype(F32) for axis in range(3)]
        here = jnp.where(pair < 8, ids[0], jnp.where(pair < 36, ids[1], ids[2]))
        place = jnp.where(row == j, here, place)
    angle = place * frequency
    even = lax.rem(lane, 2) == 0
    cosine = jnp.cos(angle)
    sine = jnp.sin(angle)
    sine = jnp.where(even, -sine, sine)
    ftmp[...] = jnp.zeros_like(ftmp)
    for j in range(6):
        two = fresh_ref[j].astype(F32)
        ftmp[j : j + 1, :] = two[0:1]
        ftmp[8 + j : 9 + j, :] = two[1:2]
    for h in range(12):
        k = ftmp[0:8, h * 128 : (h + 1) * 128]
        swapped = jnp.where(even, pltpu.roll(k, 127, 1), pltpu.roll(k, 1, 1))
        turned = k * cosine + swapped * sine
        v = ftmp[8:16, h * 128 : (h + 1) * 128]
        fbuf[y, x, :, h * 128 : (h + 1) * 128] = jnp.concatenate([turned, v], axis=0).astype(BF16)

    pl.semaphore_wait(barrier, len(greeted))

    first("fresh")
    first("out")

    length = len_ref[z]
    key_place = lax.broadcasted_iota(jnp.int32, (8, 768), 1)
    new_place = lax.broadcasted_iota(jnp.int32, (8, 128), 1)

    def mark(k, carry):
        replaced, slots = carry
        for j in range(6):
            slot = slot_ref[0, k * 6 + j]
            replaced = jnp.where(key_place == slot, 1, replaced)
            slots = jnp.where(new_place == k * 8 + j, slot, slots)
        return replaced, slots

    replaced, slots = lax.fori_loop(
        0, 16, mark, (jnp.zeros((8, 768), jnp.int32), jnp.full((8, 128), -1, jnp.int32))
    )
    bias_img = jnp.where((key_place < length) & (replaced == 0), 0.0, NEG).astype(F32)[0:1]
    bias_new = jnp.where((slots >= 0) & (slots < length), 0.0, NEG).astype(F32)[0:1]

    def cached_heads(*heads):
        if "attn" in SKIP:
            return
        for h in heads:
            cols = pl.ds(h * 128, 128)
            q = q_ref[:, cols]
            st = nt_dot(q, text[0, :, cols]) * SCALE
            si = nt_dot(q, img[0, :, cols]) * SCALE + bias_img
            m = jnp.maximum(jnp.max(st, axis=-1, keepdims=True), jnp.max(si, axis=-1, keepdims=True))
            pt = jnp.exp(st - m)
            pi = jnp.exp(si - m)
            total = jnp.sum(pt, axis=-1, keepdims=True) + jnp.sum(pi, axis=-1, keepdims=True)
            o = nn_dot(pt.astype(BF16), text[1, :, cols]) + nn_dot(pi.astype(BF16), img[1, :, cols])
            att_o[h] = o
            att_m[h] = jnp.broadcast_to(m, (48, 128))
            att_l[h] = jnp.broadcast_to(total, (48, 128))

    def fresh_heads(*heads):
        if "attn" in SKIP:
            return
        for h in heads:
            cols = pl.ds(h * 128, 128)
            q = q_ref[:, cols]
            kv = fbuf[:, :, :, cols].astype(F32)
            kf = kv[:, :, :8].reshape(128, 128).astype(BF16)
            vf = kv[:, :, 8:].reshape(128, 128).astype(BF16)
            sf = nt_dot(q, kf) * SCALE + bias_new
            before = att_m[h][:, 0:1]
            m = jnp.maximum(before, jnp.max(sf, axis=-1, keepdims=True))
            pf = jnp.exp(sf - m)
            keep = jnp.exp(before - m)
            total = att_l[h][:, 0:1] * keep + jnp.sum(pf, axis=-1, keepdims=True)
            o = att_o[h] * keep + nn_dot(pf.astype(BF16), vf)
            abuf[z, :, cols] = (o / total).astype(BF16)

    def project(*steps):
        if "proj" in SKIP:
            return
        for step in steps:
            r = ring8(step)
            rows = nn_dot(abuf[r], obuf[...].reshape(1536, 384))
            gate = mod[r, 0:1, pl.ds(pl.multiple_of(z * 384, 128), 384)]
            rbuf[z, (step + 1) % 8] = (stream[r].astype(F32) + gate * rows).astype(BF16)

    def normalize(r, carry):
        parts = [rbuf[b, lax.rem(r - b + 9, 8)].astype(F32) for b in range(8)]
        row_sum = sum(jnp.sum(p, axis=-1, keepdims=True) for p in parts)
        average = row_sum * (1.0 / 3072.0)
        centered = [p - average for p in parts]
        spread = sum(jnp.sum(p * p, axis=-1, keepdims=True) for p in centered) * (1.0 / 3072.0)
        inverse = lax.rsqrt(spread + EPSILON)
        for b in range(8):
            cols = pl.ds(b * 384, 384)
            gain = 1.0 + mod[r, 2:3, cols]
            shift = mod[r, 1:2, cols]
            nbuf[r, :, cols] = (centered[b] * inverse * gain + shift).astype(BF16)
        return carry

    def up_half(half):
        def tile(t, carry):
            cols = pl.ds(pl.multiple_of(t * 256, 256), 256)
            weights = ubuf[half, :, :, :, :, cols].reshape(3072, 256)
            pre = nn_dot(nbuf[...].reshape(384, 3072), weights)
            actbuf[half, :, cols] = jax.nn.gelu(pre, approximate=True).astype(BF16)
            return carry

        if "mm" not in SKIP:
            lax.fori_loop(0, 3, tile, 0)

    def down_half(half):
        def tile(t, carry):
            cols = pl.ds(pl.multiple_of(t * 768, 256), 768)
            rows = nt_dot(actbuf[half], dbuf[half, t].reshape(768, 768)).reshape(8, 48, 768)
            if half == 0:
                mlp[:, :, cols] = rows
            else:
                rows = rows + mlp[:, :, cols]
                gated = (rows * mod[:, 3:4, cols]).astype(BF16).reshape(384, 768)
                vel[:, :, 0:64] += nt_dot(gated, wf[:, cols]).reshape(8, 48, 64)
            return carry

        if "mm" not in SKIP:
            lax.fori_loop(0, 4, tile, 0)

    for name in ("q", "tk", "ik", "tv", "iv"):
        loads[name].wait()
    cached_heads(0, 1, 2)
    second("fresh")
    first("up0")
    cached_heads(3, 4, 5)
    third("fresh")
    second("out")
    first("up1")
    cached_heads(6, 7, 8)
    third("out")
    second("up0")
    first("down0")
    cached_heads(9, 10, 11)
    fourth("fresh")
    third("up0")
    second("up1")
    fifth("fresh")
    fresh_heads(0, 1, 2, 3, 4, 5)
    ring_go(0, 0, "R1", "L1")
    fresh_heads(6, 7, 8, 9, 10, 11)
    ring_go(0, 1, "R1", "L1")
    fourth("out")
    third("up1")
    second("down0")
    first("down1")
    hop(0, 0, 1)
    hop(0, 1, 1)
    fifth("out")
    loads["stream"].wait()
    loads["mod"].wait()
    take("out")
    project(0)
    third("down0")
    hop(0, 0, 2)
    hop(0, 1, 2)
    project(-1, 1)
    second("down1")
    fourth("up0")
    hop(0, 0, 3)
    hop(0, 1, 3)
    project(2)
    ring_go(1, 0, "R1", "L1")
    project(-2)
    third("down1")
    hop(0, 0, 4)
    hop(0, 1, 4)
    project(3, 4, -3)
    ring_go(1, 1, "R1", "L1")
    fifth("up0")
    fourth("up1")
    hop(1, 0, 1)
    hop(1, 1, 1)
    fifth("up1")
    hop(1, 0, 2)
    hop(1, 1, 2)
    fourth("down0")
    hop(1, 0, 3)
    hop(1, 1, 3)
    fifth("down0")
    loads["wf"].wait()
    vel[...] = jnp.zeros_like(vel)
    hop(1, 0, 4)
    hop(1, 1, 4)
    fourth("down1")
    if "norm" not in SKIP:
        lax.fori_loop(0, 8, normalize, 0)
    own = jnp.concatenate([rbuf[b, lax.rem(z - b + 9, 8)] for b in range(8)], axis=-1)
    vel[z, :, 0:64] = nt_dot(own, wf[...])
    take("up0")
    up_half(0)
    take("up1")
    up_half(1)
    fifth("down1")
    take("down0")
    down_half(0)
    take("down1")
    down_half(1)

    even_core = c == 0
    scale = jnp.where(even_core, GUIDANCE, 1.0 - GUIDANCE)
    for r in range(8):
        evens = vel[r, pl.ds(0, 24, stride=2), :] * scale
        odds = vel[r, pl.ds(1, 24, stride=2), :] * scale
        part[r] = jnp.where(even_core, evens, odds)
        swap_out[r] = jnp.where(even_core, odds, evens)
    swap = pltpu.make_async_remote_copy(
        src_ref=swap_out,
        dst_ref=swap_in,
        send_sem=send_sem.at[N_COPY - 1],
        recv_sem=recv_sem.at[N_COPY - 1],
        device_id={"cfg": 1 - c},
        device_id_type=MESH,
    )
    swap.start()
    started.append(swap)
    swap.wait_recv()
    part[...] = part[...] + swap_in[...]

    def velocity_copy(step):
        target = ring8(step)
        index = N_PLANE + N_RING + step
        return pltpu.make_async_remote_copy(
            src_ref=part.at[target],
            dst_ref=partin.at[step],
            send_sem=send_sem.at[index],
            recv_sem=recv_sem.at[index],
            device_id={"req": target},
            device_id_type=MESH,
        )

    for step in (4, 3, 5, 2, 6, 1, 7):
        velocity_copy(step).start()
        started.append(velocity_copy(step))
    index = jnp.full((24, 64), step_ref[0], jnp.int32)
    now = noise_level(index)
    later = noise_level(index + 1)
    token = s * 48 + 2 * lax.broadcasted_iota(jnp.int32, (24, 64), 0) + c
    valid = token < length
    current = lat_ref[...]
    guided = part[z]
    for step in range(1, 8):
        velocity_copy(step).wait_recv()
        guided = guided + partin[step]
    guided = guided[:, 0:64]
    res_ref[0] = jnp.where(valid, current + (later - now) * guided, current)
    res_ref[1] = jnp.where(valid, current - now * guided, current)

    def finish(core):
        for item, op in plane_log:
            plane(item, op, core).wait_send()

    both(finish)
    for copy in started:
        copy.wait_send()


def per_device(
    queries,
    text_cache,
    image_cache,
    fresh_kv,
    fresh_slots,
    fresh_pos,
    image_len,
    stream,
    modulation,
    out_weight,
    up_weight,
    down_weight,
    final_weight,
    latent,
    step_index,
):
    vmem = pl.BlockSpec(memory_space=pltpu.VMEM)
    smem = pl.BlockSpec(memory_space=pltpu.SMEM)
    hbm = pl.BlockSpec(memory_space=pl.ANY)
    both = pl.pallas_call(
        kernel,
        out_shape=jax.ShapeDtypeStruct((2, 24, 64), F32),
        in_specs=[smem] * 4 + [hbm] * 3 + [vmem] + [hbm] * 6 + [vmem],
        out_specs=vmem,
        scratch_shapes=[
            pltpu.VMEM((48, 1536), BF16),
            pltpu.VMEM((2, 512, 1536), BF16),
            pltpu.VMEM((2, 768, 1536), BF16),
            pltpu.VMEM((8, 48, 384), BF16),
            pltpu.VMEM((8, 4, 3072), F32),
            pltpu.VMEM((64, 3072), BF16),
            pltpu.VMEM((16, 1536), F32),
            pltpu.VMEM((4, 4, 16, 1536), BF16),
            pltpu.VMEM((4, 4, 2, 48, 384), BF16),
            pltpu.VMEM((2, 4, 4, 2, 96, 768), BF16),
            pltpu.VMEM((2, 4, 4, 2, 96, 768), BF16),
            pltpu.VMEM((8, 48, 1536), BF16),
            pltpu.VMEM((8, 8, 48, 384), BF16),
            pltpu.VMEM((8, 48, 3072), BF16),
            pltpu.VMEM((2, 384, 768), BF16),
            pltpu.VMEM((8, 48, 3072), F32),
            pltpu.VMEM((12, 48, 128), F32),
            pltpu.VMEM((12, 48, 128), F32),
            pltpu.VMEM((12, 48, 128), F32),
            pltpu.VMEM((8, 48, 128), F32),
            pltpu.VMEM((8, 24, 128), F32),
            pltpu.VMEM((8, 24, 128), F32),
            pltpu.VMEM((8, 24, 128), F32),
            pltpu.VMEM((8, 24, 128), F32),
            pltpu.SemaphoreType.DMA((13,)),
            pltpu.SemaphoreType.DMA((N_COPY,)),
            pltpu.SemaphoreType.DMA((N_COPY,)),
        ],
        compiler_params=pltpu.CompilerParams(
            collective_id=0, has_side_effects=True, vmem_limit_bytes=60 * 1024 * 1024
        ),
    )(
        image_len,
        step_index,
        fresh_slots,
        fresh_pos,
        queries[0, 0],
        text_cache[0, 0],
        image_cache[0, 0],
        fresh_kv[0, 0].transpose(1, 0, 2),
        stream[0],
        modulation,
        out_weight.reshape(2, 48, 384),
        up_weight.reshape(2, 96, 1536),
        down_weight.T.reshape(2, 96, 1536),
        final_weight.T,
        latent[0],
    )
    return (both[0][None], both[1][None])


def solution(mesh):
    in_specs = (
        P("cfg", "req", "seq", None),
        P("cfg", "req", None, None, None),
        P("cfg", "req", None, None, None),
        P("cfg", "req", None, "seq", None),
        P("req", None),
        P(None, "req", "seq"),
        P(),
        P("cfg", None, "seq", "req"),
        P(),
        P("seq", "req"),
        P("seq", "req"),
        P("req", "seq"),
        P(),
        P("req", "seq", "cfg"),
        P(),
    )
    out_specs = (P("req", "seq", "cfg"), P("req", "seq", "cfg"))
    return jax.shard_map(
        per_device, mesh=mesh, in_specs=in_specs, out_specs=out_specs, check_vma=False
    )
```

```python
import functools
import math

import jax
import jax.numpy as jnp
from jax import lax
from jax.experimental import pallas as pl
from jax.experimental.pallas import tpu as pltpu
from jax.sharding import PartitionSpec as P

STEPS = 28
GUIDANCE = 3.0
SHIFT = 3.0
SCALE = 1.0 / math.sqrt(128.0)
EPSILON = 1e-06
MESH = pl.DeviceIdType.MESH
F32 = jnp.float32
BF16 = jnp.bfloat16
NEG = -jnp.inf
SKIP = frozenset()

ITEMS = ("fresh", "out", "up0", "up1")
OPS = ("1R", "1L", "1RR", "1LL", "2R", "2L", "2RR", "2LL", "Xa", "Xb", "Xc", "Ya", "Yb", "Yc")
N_PLANE = len(ITEMS) * len(OPS)
RING_OPS = ("R1", "R2", "R3", "R4", "L1", "L2", "L3", "L4")
N_RING = 4 * len(RING_OPS)
N_VEL = 8
FOLD_OPS = ("1R", "1L", "2R", "2L", "3R", "3L", "4R", "4L", "5R", "5L", "5RR", "5LL", "6R", "6L", "6RR", "6LL")
N_FOLD = len(FOLD_OPS)
N_COPY = N_PLANE + N_RING + N_VEL + N_FOLD + 1


def nt_dot(a, b):
    return lax.dot_general(a, b, (((1,), (1,)), ((), ())), preferred_element_type=F32)


def nn_dot(a, b):
    return jnp.dot(a, b, preferred_element_type=F32)


def noise_level(index):
    fraction = 1.0 - index.astype(F32) / STEPS
    return SHIFT * fraction / (SHIFT * fraction + 1.0 - fraction)


def kernel(
    len_ref,
    step_ref,
    slot_ref,
    pos_ref,
    q_hbm,
    text_hbm,
    img_hbm,
    fresh_ref,
    stream_hbm,
    mod_hbm,
    out_hbm,
    up_hbm,
    down_hbm,
    wf_hbm,
    lat_ref,
    res_ref,
    q_ref,
    text,
    img,
    stream,
    mod,
    wf,
    ftmp,
    fbuf,
    obuf,
    ubuf,
    down,
    gpart,
    gmid,
    gfull,
    gin1,
    gin2,
    gin3,
    gin4,
    abuf,
    rbuf,
    nbuf,
    actbuf,
    att_o,
    att_m,
    att_l,
    vel,
    swap_out,
    swap_in,
    part,
    partin,
    load_sem,
    send_sem,
    recv_sem,
):
    c = lax.axis_index("cfg")
    z = lax.axis_index("req")
    s = lax.axis_index("seq")
    y = s // 4
    x = s % 4

    def ring8(i):
        return lax.rem(z + i + 8, 8)

    started = []

    loads = {}

    def load(name, src, dst):
        loads[name] = pltpu.make_async_copy(src, dst, load_sem.at[len(loads)])
        loads[name].start()

    load("q", q_hbm, q_ref)
    load("tk", text_hbm.at[0], text.at[0])
    load("ik", img_hbm.at[0], img.at[0])
    load("tv", text_hbm.at[1], text.at[1])
    load("iv", img_hbm.at[1], img.at[1])
    load("out", out_hbm, obuf.at[y, x])
    for half in (0, 1):
        load("up%d" % half, up_hbm.at[:, :, pl.ds(768 * half, 768)], ubuf.at[half, y, x])
    load("down", down_hbm, down)
    load("stream", stream_hbm, stream)
    load("mod", mod_hbm.at[c], mod)
    load("wf", wf_hbm, wf)

    def plane(item, op, core):
        half = int(item[-1]) if item[-1] in "01" else 0
        if item == "fresh":
            buf, shard = fbuf, None
        elif item == "out":
            buf, shard = obuf, out_hbm.at[core]
        else:
            buf, shard = ubuf.at[half], up_hbm.at[core, :, pl.ds(768 * half, 768)]
        u, v = (x, y) if core == 0 else (y, x)
        own = () if item == "fresh" else (core,)

        def mod4(i):
            return lax.rem(i + 4, 4)

        def at(uu, vv, extra=()):
            where = (vv, uu) if core == 0 else (uu, vv)
            return buf.at[where + own + extra]

        def device(uu, vv):
            return {"seq": vv * 4 + uu if core == 0 else uu * 4 + vv}

        if item == "fresh":
            halves = ((slice(None), pl.ds(0, 768)), (slice(None), pl.ds(768, 768)))
        elif item == "out":
            halves = ((pl.ds(0, 32),), (pl.ds(32, 16),))
        else:
            halves = ((pl.ds(0, 48),), (pl.ds(48, 48),))
        right1, left1 = device(mod4(u + 1), v), device(mod4(u - 1), v)
        right2, left2 = device(u, mod4(v + 1)), device(u, mod4(v - 1))
        every = slice(None)
        if op in ("1R", "1L"):
            dst = at(u, v)
            src = dst if item == "fresh" else shard
            dev = right1 if op == "1R" else left1
        elif op == "1RR":
            src = dst = at(mod4(u - 1), v, halves[0])
            dev = right1
        elif op == "1LL":
            src = dst = at(mod4(u + 1), v, halves[1])
            dev = left1
        elif op in ("2R", "2L"):
            src = dst = at(every, v)
            dev = right2 if op == "2R" else left2
        elif op == "2RR":
            src = dst = at(pl.ds(0, 2), mod4(v - 1))
            dev = right2
        elif op == "2LL":
            src = dst = at(pl.ds(2, 2), mod4(v + 1))
            dev = left2
        else:
            step = {"a": -1, "b": 1, "c": 2}[op[1]]
            src = dst = at(mod4(u + step), v) if op[0] == "X" else at(every, mod4(v + step))
            dev = {"cfg": 1 - core}
        index = ITEMS.index(item) * len(OPS) + OPS.index(op)
        return pltpu.make_async_remote_copy(
            src_ref=src,
            dst_ref=dst,
            send_sem=send_sem.at[index],
            recv_sem=recv_sem.at[index],
            device_id=dev,
            device_id_type=MESH,
        )

    plane_log = []

    def both(act):
        for core in (0, 1):
            pl.when(c == core)(functools.partial(act, core))

    def serve(*steps):
        steps = [step for step in steps if step[0] not in SKIP]
        for item, _, after in steps:
            plane_log.extend((item, op) for op in after.split())

        def act(core):
            for item, op, after in steps:
                if op:
                    plane(item, op, core).wait_recv()
                for follow in after.split():
                    plane(item, follow, core).start()

        if steps:
            both(act)

    def first(item):
        serve((item, None, "1R 1L"))

    def second(item):
        hand = item != "fresh"
        serve((item, "1R", "1RR Xa" if hand else "1RR"), (item, "1L", "1LL Xb" if hand else "1LL"))

    def third(item):
        if item in loads:
            loads[item].wait()
        hand = item != "fresh"
        serve((item, "1RR", ""), (item, "1LL", "2R 2L Xc" if hand else "2R 2L"))

    def fourth(item):
        hand = item != "fresh"
        serve((item, "2R", "2RR Ya" if hand else "2RR"), (item, "2L", "2LL Yb" if hand else "2LL"))

    def fifth(item):
        hand = item != "fresh"
        serve((item, "2RR", ""), (item, "2LL", "Yc" if hand else ""))

    def take(item):
        if item in SKIP:
            return

        def act(core):
            for op in ("Xa", "Xb", "Xc", "Ya", "Yb", "Yc"):
                plane(item, op, 1 - core).wait_recv()

        both(act)

    def fold(op, core):
        u, v = (x, y) if core == 0 else (y, x)

        def mod4(i):
            return lax.rem(i + 4, 4)

        right = "R" in op
        one = 1 if right else -1
        along_u = op[0] in "126"
        uu, vv = (mod4(u + one), v) if along_u else (u, mod4(v + one))
        dev = {"seq": vv * 4 + uu if core == 0 else uu * 4 + vv}
        side = 0 if right else 1
        if op[0] == "1":
            src, dst = gpart.at[mod4(u + 2), pl.ds(2 * side, 2)], gin1.at[side]
        elif op[0] == "2":
            src, dst = gpart.at[mod4(u + one)], gin2.at[side]
        elif op[0] == "3":
            src, dst = gmid.at[mod4(v + 2), pl.ds(16 * side, 16)], gin3.at[side]
        elif op[0] == "4":
            src, dst = gmid.at[mod4(v + one)], gin4.at[side]
        elif op[0] == "5":
            src = gfull.at[u, v] if len(op) == 2 else gfull.at[u, mod4(v - one), pl.ds(16 * side, 16)]
            dst = src
        else:
            src = gfull.at[u] if len(op) == 2 else gfull.at[mod4(u - one), pl.ds(2 * side, 2)]
            dst = src
        index = N_PLANE + N_RING + N_VEL + FOLD_OPS.index(op)
        return pltpu.make_async_remote_copy(
            src_ref=src,
            dst_ref=dst,
            send_sem=send_sem.at[index],
            recv_sem=recv_sem.at[index],
            device_id=dev,
            device_id_type=MESH,
        )

    fold_log = []

    def fold_step(*steps):
        if "fold" in SKIP:
            return
        for _, _, after in steps:
            fold_log.extend(after.split())

        def act(core):
            for op, add, after in steps:
                if op:
                    fold(op, core).wait_recv()
                if add:
                    add(core)
                for follow in after.split():
                    fold(follow, core).start()

        both(act)

    def across(core, step):
        u, v = (x, y) if core == 0 else (y, x)
        return lax.rem(u + step + 4, 4), lax.rem(v + step + 4, 4)

    def add1(side):
        def add(core):
            u = across(core, 1 - 2 * side)[0]
            for i in range(2):
                place = 2 * side + i
                total = gpart[u, place].astype(F32) + gin1[side, i].astype(F32)
                gpart[u, place] = total.astype(BF16)

        return add

    def add2(core):
        u = across(core, 0)[0]
        for i in range(4):
            total = gpart[u, i].astype(F32) + gin2[0, i].astype(F32) + gin2[1, i].astype(F32)
            gmid[i] = total.astype(BF16)

    def add3(side):
        def add(core):
            v = across(core, 1 - 2 * side)[1]
            rows = pl.ds(16 * side, 16)
            gmid[v, rows] = (gmid[v, rows].astype(F32) + gin3[side].astype(F32)).astype(BF16)

        return add

    def add4(core):
        u, v = across(core, 0)
        total = gmid[v].astype(F32) + gin4[0].astype(F32) + gin4[1].astype(F32)
        gfull[u, v] = total.astype(BF16)

    def fold_local():
        if "fold" in SKIP:
            return
        window = pl.ds(pl.multiple_of((s // 2) * 384, 128), 384)
        odd = s % 2 == 1

        def mine(block):
            return jnp.where(odd, pltpu.roll(block, 192, 1), block)[:, 0:192]

        final = mine(wf[:, window].astype(F32))
        down_rows = down[...].reshape(192, 1536)
        for r in range(8):
            gate = mine(jnp.broadcast_to(mod[r, 3:4, window], (8, 384)))[0:1]
            product = nn_dot((final * gate).astype(BF16), down_rows)
            gpart[r // 2, 2 * (r % 2)] = product[0:32].astype(BF16)
            gpart[r // 2, 2 * (r % 2) + 1] = product[32:64].astype(BF16)

    def ring(which, chunk, op):
        k = int(op[1])
        right = op[0] == "R"
        owner = ring8(1 - k if right else k - 1)
        if which == 0:
            src = abuf.at[owner, :, pl.ds(768 * chunk, 768)]
        else:
            src = rbuf.at[owner, pl.ds(4 * chunk, 4)]
        index = N_PLANE + (which * 2 + chunk) * len(RING_OPS) + RING_OPS.index(op)
        return pltpu.make_async_remote_copy(
            src_ref=src,
            dst_ref=src,
            send_sem=send_sem.at[index],
            recv_sem=recv_sem.at[index],
            device_id={"req": ring8(1 if right else -1)},
            device_id_type=MESH,
        )

    def ring_go(which, chunk, *ops):
        for op in ops:
            if "ring%d" % which not in SKIP:
                ring(which, chunk, op).start()
                started.append(ring(which, chunk, op))

    def hop(which, chunk, k):
        if "ring%d" % which in SKIP:
            return
        for side in "RL":
            if k < 4 or chunk == "RL".index(side):
                ring(which, chunk, side + str(k)).wait_recv()
            if k < 3 or (k == 3 and chunk == "RL".index(side)):
                ring_go(which, chunk, side + str(k + 1))

    barrier = pltpu.get_barrier_semaphore()
    greeted = [{"cfg": 1 - c}]
    for step in (1, 3):
        greeted.append({"seq": y * 4 + lax.rem(x + step, 4)})
        greeted.append({"seq": lax.rem(y + step, 4) * 4 + x})
    for step in range(1, 8):
        greeted.append({"req": ring8(step)})
    for device in greeted:
        pl.semaphore_signal(barrier, inc=1, device_id=device, device_id_type=MESH)

    lane = lax.broadcasted_iota(jnp.int32, (8, 128), 1)
    row = lax.broadcasted_iota(jnp.int32, (8, 128), 0)
    pair = lane // 2
    offset = jnp.where(pair < 8, 0, jnp.where(pair < 36, 8, 36))
    span = jnp.where(pair < 8, 16.0, 56.0)
    frequency = jnp.exp(-(2.0 * (pair - offset).astype(F32) / span) * math.log(10000.0))
    place = jnp.zeros((8, 128), F32)
    for j in range(6):
        ids = [jnp.full((8, 128), pos_ref[axis, 0, j], jnp.int32).astype(F32) for axis in range(3)]
        here = jnp.where(pair < 8, ids[0], jnp.where(pair < 36, ids[1], ids[2]))
        place = jnp.where(row == j, here, place)
    angle = place * frequency
    even = lax.rem(lane, 2) == 0
    cosine = jnp.cos(angle)
    sine = jnp.sin(angle)
    sine = jnp.where(even, -sine, sine)
    ftmp[...] = jnp.zeros_like(ftmp)
    for j in range(6):
        two = fresh_ref[j].astype(F32)
        ftmp[j : j + 1, :] = two[0:1]
        ftmp[8 + j : 9 + j, :] = two[1:2]
    for h in range(12):
        k = ftmp[0:8, h * 128 : (h + 1) * 128]
        swapped = jnp.where(even, pltpu.roll(k, 127, 1), pltpu.roll(k, 1, 1))
        turned = k * cosine + swapped * sine
        v = ftmp[8:16, h * 128 : (h + 1) * 128]
        fbuf[y, x, :, h * 128 : (h + 1) * 128] = jnp.concatenate([turned, v], axis=0).astype(BF16)

    pl.semaphore_wait(barrier, len(greeted))

    first("fresh")
    first("out")

    length = len_ref[z]
    key_place = lax.broadcasted_iota(jnp.int32, (8, 768), 1)
    new_place = lax.broadcasted_iota(jnp.int32, (8, 128), 1)

    def mark(k, carry):
        replaced, slots = carry
        for j in range(6):
            slot = slot_ref[0, k * 6 + j]
            replaced = jnp.where(key_place == slot, 1, replaced)
            slots = jnp.where(new_place == k * 8 + j, slot, slots)
        return replaced, slots

    replaced, slots = lax.fori_loop(
        0, 16, mark, (jnp.zeros((8, 768), jnp.int32), jnp.full((8, 128), -1, jnp.int32))
    )
    bias_img = jnp.where((key_place < length) & (replaced == 0), 0.0, NEG).astype(F32)[0:1]
    bias_new = jnp.where((slots >= 0) & (slots < length), 0.0, NEG).astype(F32)[0:1]

    def cached_heads(*heads):
        if "attn" in SKIP:
            return
        for h in heads:
            cols = pl.ds(h * 128, 128)
            q = q_ref[:, cols]
            st = nt_dot(q, text[0, :, cols]) * SCALE
            si = nt_dot(q, img[0, :, cols]) * SCALE + bias_img
            m = jnp.maximum(jnp.max(st, axis=-1, keepdims=True), jnp.max(si, axis=-1, keepdims=True))
            pt = jnp.exp(st - m)
            pi = jnp.exp(si - m)
            total = jnp.sum(pt, axis=-1, keepdims=True) + jnp.sum(pi, axis=-1, keepdims=True)
            o = nn_dot(pt.astype(BF16), text[1, :, cols]) + nn_dot(pi.astype(BF16), img[1, :, cols])
            att_o[h] = o
            att_m[h] = jnp.broadcast_to(m, (48, 128))
            att_l[h] = jnp.broadcast_to(total, (48, 128))

    def fresh_heads(*heads):
        if "attn" in SKIP:
            return
        for h in heads:
            cols = pl.ds(h * 128, 128)
            q = q_ref[:, cols]
            kv = fbuf[:, :, :, cols].astype(F32)
            kf = kv[:, :, :8].reshape(128, 128).astype(BF16)
            vf = kv[:, :, 8:].reshape(128, 128).astype(BF16)
            sf = nt_dot(q, kf) * SCALE + bias_new
            before = att_m[h][:, 0:1]
            m = jnp.maximum(before, jnp.max(sf, axis=-1, keepdims=True))
            pf = jnp.exp(sf - m)
            keep = jnp.exp(before - m)
            total = att_l[h][:, 0:1] * keep + jnp.sum(pf, axis=-1, keepdims=True)
            o = att_o[h] * keep + nn_dot(pf.astype(BF16), vf)
            abuf[z, :, cols] = (o / total).astype(BF16)

    def project(*steps):
        if "proj" in SKIP:
            return
        for step in steps:
            r = ring8(step)
            rows = nn_dot(abuf[r], obuf[...].reshape(1536, 384))
            gate = mod[r, 0:1, pl.ds(pl.multiple_of(z * 384, 128), 384)]
            rbuf[z, (step + 1) % 8] = (stream[r].astype(F32) + gate * rows).astype(BF16)

    def normalize(r, carry):
        parts = [rbuf[b, lax.rem(r - b + 9, 8)].astype(F32) for b in range(8)]
        row_sum = sum(jnp.sum(p, axis=-1, keepdims=True) for p in parts)
        average = row_sum * (1.0 / 3072.0)
        centered = [p - average for p in parts]
        spread = sum(jnp.sum(p * p, axis=-1, keepdims=True) for p in centered) * (1.0 / 3072.0)
        inverse = lax.rsqrt(spread + EPSILON)
        for b in range(8):
            cols = pl.ds(b * 384, 384)
            gain = 1.0 + mod[r, 2:3, cols]
            shift = mod[r, 1:2, cols]
            nbuf[r, :, cols] = (centered[b] * inverse * gain + shift).astype(BF16)
        return carry

    def up_half(half):
        def tile(t, carry):
            cols = pl.ds(pl.multiple_of(t * 256, 256), 256)
            weights = ubuf[half, :, :, :, :, cols].reshape(3072, 256)
            pre = nn_dot(nbuf[...].reshape(384, 3072), weights)
            actbuf[half, :, cols] = jax.nn.gelu(pre, approximate=True).astype(BF16)
            return carry

        if "mm" not in SKIP:
            lax.fori_loop(0, 3, tile, 0)

    def velocity(r, carry):
        fold_r = gfull[lax.div(r, 2), pl.ds(2 * lax.rem(r, 2), 2)].reshape(64, 1536)
        rows = nt_dot(actbuf[0, pl.ds(r * 48, 48)], fold_r[:, 0:768])
        rows += nt_dot(actbuf[1, pl.ds(r * 48, 48)], fold_r[:, 768:1536])
        vel[r, :, 0:64] += rows
        return carry

    for name in ("q", "tk", "ik", "tv", "iv"):
        loads[name].wait()
    cached_heads(0, 1, 2)
    second("fresh")
    first("up0")
    cached_heads(3, 4, 5)
    third("fresh")
    second("out")
    first("up1")
    cached_heads(6, 7, 8)
    third("out")
    second("up0")
    cached_heads(9, 10, 11)
    fourth("fresh")
    third("up0")
    second("up1")
    fifth("fresh")
    fresh_heads(0, 1, 2, 3, 4, 5)
    ring_go(0, 0, "R1", "L1")
    fresh_heads(6, 7, 8, 9, 10, 11)
    ring_go(0, 1, "R1", "L1")
    fourth("out")
    third("up1")
    for name in ("stream", "mod", "wf", "down"):
        loads[name].wait()
    hop(0, 0, 1)
    hop(0, 1, 1)
    fifth("out")
    fold_local()
    fold_step((None, None, "1R 1L"))
    take("out")
    project(0)
    hop(0, 0, 2)
    hop(0, 1, 2)
    project(-1, 1)
    fourth("up0")
    hop(0, 0, 3)
    hop(0, 1, 3)
    project(2)
    ring_go(1, 0, "R1", "L1")
    project(-2)
    fold_step(("1R", add1(0), "2R"), ("1L", add1(1), "2L"))
    hop(0, 0, 4)
    hop(0, 1, 4)
    project(3, 4, -3)
    ring_go(1, 1, "R1", "L1")
    fifth("up0")
    fourth("up1")
    hop(1, 0, 1)
    hop(1, 1, 1)
    fold_step(("2R", None, ""), ("2L", add2, "3R 3L"))
    hop(1, 0, 2)
    fold_step(("3R", add3(0), "4R"), ("3L", add3(1), "4L"))
    hop(1, 1, 2)
    fold_step(("4R", None, ""), ("4L", add4, "5R 5L"))
    fifth("up1")
    vel[...] = jnp.zeros_like(vel)
    hop(1, 0, 3)
    fold_step(("5R", None, "5RR"), ("5L", None, "5LL"))
    hop(1, 1, 3)
    fold_step(("5RR", None, ""), ("5LL", None, "6R 6L"))
    hop(1, 0, 4)
    hop(1, 1, 4)
    if "norm" not in SKIP:
        lax.fori_loop(0, 8, normalize, 0)
    fold_step(("6R", None, "6RR"), ("6L", None, "6LL"))
    own = jnp.concatenate([rbuf[b, lax.rem(z - b + 9, 8)] for b in range(8)], axis=-1)
    vel[z, :, 0:64] = nt_dot(own, wf[...])
    take("up0")
    up_half(0)
    take("up1")
    up_half(1)
    fold_step(("6RR", None, ""), ("6LL", None, ""))
    if "mm" not in SKIP:
        lax.fori_loop(0, 8, velocity, 0)

    even_core = c == 0
    scale = jnp.where(even_core, GUIDANCE, 1.0 - GUIDANCE)
    for r in range(8):
        evens = vel[r, pl.ds(0, 24, stride=2), :] * scale
        odds = vel[r, pl.ds(1, 24, stride=2), :] * scale
        part[r] = jnp.where(even_core, evens, odds)
        swap_out[r] = jnp.where(even_core, odds, evens)
    swap = pltpu.make_async_remote_copy(
        src_ref=swap_out,
        dst_ref=swap_in,
        send_sem=send_sem.at[N_COPY - 1],
        recv_sem=recv_sem.at[N_COPY - 1],
        device_id={"cfg": 1 - c},
        device_id_type=MESH,
    )
    swap.start()
    started.append(swap)
    swap.wait_recv()
    part[...] = part[...] + swap_in[...]

    def velocity_copy(step):
        target = ring8(step)
        index = N_PLANE + N_RING + step
        return pltpu.make_async_remote_copy(
            src_ref=part.at[target],
            dst_ref=partin.at[step],
            send_sem=send_sem.at[index],
            recv_sem=recv_sem.at[index],
            device_id={"req": target},
            device_id_type=MESH,
        )

    for step in (4, 3, 5, 2, 6, 1, 7):
        velocity_copy(step).start()
        started.append(velocity_copy(step))
    index = jnp.full((24, 64), step_ref[0], jnp.int32)
    now = noise_level(index)
    later = noise_level(index + 1)
    token = s * 48 + 2 * lax.broadcasted_iota(jnp.int32, (24, 64), 0) + c
    valid = token < length
    current = lat_ref[...]
    guided = part[z]
    for step in range(1, 8):
        velocity_copy(step).wait_recv()
        guided = guided + partin[step]
    guided = guided[:, 0:64]
    res_ref[0] = jnp.where(valid, current + (later - now) * guided, current)
    res_ref[1] = jnp.where(valid, current - now * guided, current)

    def finish(core):
        for item, op in plane_log:
            plane(item, op, core).wait_send()
        for op in fold_log:
            fold(op, core).wait_send()

    both(finish)
    for copy in started:
        copy.wait_send()


def per_device(
    queries,
    text_cache,
    image_cache,
    fresh_kv,
    fresh_slots,
    fresh_pos,
    image_len,
    stream,
    modulation,
    out_weight,
    up_weight,
    down_weight,
    final_weight,
    latent,
    step_index,
):
    vmem = pl.BlockSpec(memory_space=pltpu.VMEM)
    smem = pl.BlockSpec(memory_space=pltpu.SMEM)
    hbm = pl.BlockSpec(memory_space=pl.ANY)
    both = pl.pallas_call(
        kernel,
        out_shape=jax.ShapeDtypeStruct((2, 24, 64), F32),
        in_specs=[smem] * 4 + [hbm] * 3 + [vmem] + [hbm] * 6 + [vmem],
        out_specs=vmem,
        scratch_shapes=[
            pltpu.VMEM((48, 1536), BF16),
            pltpu.VMEM((2, 512, 1536), BF16),
            pltpu.VMEM((2, 768, 1536), BF16),
            pltpu.VMEM((8, 48, 384), BF16),
            pltpu.VMEM((8, 4, 3072), F32),
            pltpu.VMEM((64, 3072), BF16),
            pltpu.VMEM((16, 1536), F32),
            pltpu.VMEM((4, 4, 16, 1536), BF16),
            pltpu.VMEM((4, 4, 2, 48, 384), BF16),
            pltpu.VMEM((2, 4, 4, 2, 96, 768), BF16),
            pltpu.VMEM((2, 96, 1536), BF16),
            pltpu.VMEM((4, 4, 32, 1536), BF16),
            pltpu.VMEM((4, 32, 1536), BF16),
            pltpu.VMEM((4, 4, 32, 1536), BF16),
            pltpu.VMEM((2, 2, 32, 1536), BF16),
            pltpu.VMEM((2, 4, 32, 1536), BF16),
            pltpu.VMEM((2, 16, 1536), BF16),
            pltpu.VMEM((2, 32, 1536), BF16),
            pltpu.VMEM((8, 48, 1536), BF16),
            pltpu.VMEM((8, 8, 48, 384), BF16),
            pltpu.VMEM((8, 48, 3072), BF16),
            pltpu.VMEM((2, 384, 768), BF16),
            pltpu.VMEM((12, 48, 128), F32),
            pltpu.VMEM((12, 48, 128), F32),
            pltpu.VMEM((12, 48, 128), F32),
            pltpu.VMEM((8, 48, 128), F32),
            pltpu.VMEM((8, 24, 128), F32),
            pltpu.VMEM((8, 24, 128), F32),
            pltpu.VMEM((8, 24, 128), F32),
            pltpu.VMEM((8, 24, 128), F32),
            pltpu.SemaphoreType.DMA((12,)),
            pltpu.SemaphoreType.DMA((N_COPY,)),
            pltpu.SemaphoreType.DMA((N_COPY,)),
        ],
        compiler_params=pltpu.CompilerParams(
            collective_id=0, has_side_effects=True, vmem_limit_bytes=60 * 1024 * 1024
        ),
    )(
        image_len,
        step_index,
        fresh_slots,
        fresh_pos,
        queries[0, 0],
        text_cache[0, 0],
        image_cache[0, 0],
        fresh_kv[0, 0].transpose(1, 0, 2),
        stream[0],
        modulation,
        out_weight.reshape(2, 48, 384),
        up_weight.reshape(2, 96, 1536),
        down_weight.T.reshape(2, 96, 1536),
        final_weight.T,
        latent[0],
    )
    return (both[0][None], both[1][None])


def solution(mesh):
    in_specs = (
        P("cfg", "req", "seq", None),
        P("cfg", "req", None, None, None),
        P("cfg", "req", None, None, None),
        P("cfg", "req", None, "seq", None),
        P("req", None),
        P(None, "req", "seq"),
        P(),
        P("cfg", None, "seq", "req"),
        P(),
        P("seq", "req"),
        P("seq", "req"),
        P("req", "seq"),
        P(),
        P("req", "seq", "cfg"),
        P(),
    )
    out_specs = (P("req", "seq", "cfg"), P("req", "seq", "cfg"))
    return jax.shard_map(
        per_device, mesh=mesh, in_specs=in_specs, out_specs=out_specs, check_vma=False
    )
```

```python
import functools
import math

import jax
import jax.numpy as jnp
from jax import lax
from jax.experimental import pallas as pl
from jax.experimental.pallas import tpu as pltpu
from jax.sharding import PartitionSpec as P

STEPS = 28
GUIDANCE = 3.0
SHIFT = 3.0
SCALE = 1.0 / math.sqrt(128.0)
EPSILON = 1e-06
MESH = pl.DeviceIdType.MESH
F32 = jnp.float32
BF16 = jnp.bfloat16
NEG = -jnp.inf
SKIP = frozenset()

ITEMS = ("out", "up0", "up1")
OPS = ("1R", "1L", "1O", "2O", "1RR", "1LL", "2R", "2L", "2RR", "2LL", "Xa", "Xb", "Xc", "Ya", "Yb", "Yc")
N_PLANE = len(ITEMS) * len(OPS)
RING_OPS = ("R1", "R2", "R3", "R4", "L1", "L2", "L3", "L4")
N_RING = 4 * len(RING_OPS)
N_VEL = 8
FOLD_OPS = ("1R", "1L", "2R", "2L", "3R", "3L", "3O", "4R", "4L", "4O", "5R", "5L", "5RR", "5LL")
N_FOLD = len(FOLD_OPS)
N_COPY = N_PLANE + N_RING + N_VEL + N_FOLD + 32 + 1


def nt_dot(a, b):
    return lax.dot_general(a, b, (((1,), (1,)), ((), ())), preferred_element_type=F32)


def nn_dot(a, b):
    return jnp.dot(a, b, preferred_element_type=F32)


def noise_level(index):
    fraction = 1.0 - index.astype(F32) / STEPS
    return SHIFT * fraction / (SHIFT * fraction + 1.0 - fraction)


def kernel(
    len_ref,
    step_ref,
    slot_ref,
    pos_ref,
    q_hbm,
    text_hbm,
    img_hbm,
    fresh_ref,
    stream_hbm,
    mod_hbm,
    out_hbm,
    up_hbm,
    down_hbm,
    wf_hbm,
    lat_ref,
    res_ref,
    q_ref,
    text,
    img,
    stream,
    mod,
    wf,
    ftmp,
    fbuf,
    obuf,
    ubuf,
    down,
    gpart,
    gmid,
    gfull,
    gin1,
    gin2,
    gin3,
    abuf,
    rbuf,
    nbuf,
    actbuf,
    att_o,
    att_m,
    att_l,
    vel,
    swap_out,
    swap_in,
    part,
    partin,
    load_sem,
    send_sem,
    recv_sem,
):
    c = lax.axis_index("cfg")
    z = lax.axis_index("req")
    s = lax.axis_index("seq")
    y = s // 4
    x = s % 4

    def ring8(i):
        return lax.rem(z + i + 8, 8)

    started = []

    loads = {}

    def load(name, src, dst):
        loads[name] = pltpu.make_async_copy(src, dst, load_sem.at[len(loads)])
        loads[name].start()

    load("mod", mod_hbm.at[c], mod)
    load("wf", wf_hbm, wf)
    load("down", down_hbm, down)
    load("q", q_hbm, q_ref)
    load("tk", text_hbm.at[0], text.at[0])
    load("ik", img_hbm.at[0], img.at[0])
    load("tv", text_hbm.at[1], text.at[1])
    load("iv", img_hbm.at[1], img.at[1])
    load("out", out_hbm, obuf.at[y, x])
    for half in (0, 1):
        load("up%d" % half, up_hbm.at[:, :, pl.ds(768 * half, 768)], ubuf.at[half, y, x])
    load("stream", stream_hbm, stream)

    def plane(item, op, core):
        half = int(item[-1]) if item[-1] in "01" else 0
        if item == "out":
            buf, shard = obuf, out_hbm.at[core]
        else:
            buf, shard = ubuf.at[half], up_hbm.at[core, :, pl.ds(768 * half, 768)]
        u, v = (x, y) if core == 0 else (y, x)
        def mod4(i):
            return lax.rem(i + 4, 4)

        def at(uu, vv, extra=()):
            where = (vv, uu) if core == 0 else (uu, vv)
            return buf.at[where + (core,) + extra]

        def device(uu, vv):
            return {"seq": vv * 4 + uu if core == 0 else uu * 4 + vv}

        if item == "out":
            halves = ((pl.ds(0, 32),), (pl.ds(32, 16),))
        else:
            halves = ((pl.ds(0, 48),), (pl.ds(48, 48),))
        right1, left1 = device(mod4(u + 1), v), device(mod4(u - 1), v)
        right2, left2 = device(u, mod4(v + 1)), device(u, mod4(v - 1))
        every = slice(None)
        if op in ("1R", "1L", "1O"):
            src, dst = shard, at(u, v)
            dev = {"R": right1, "L": left1, "O": device(mod4(u + 2), v)}[op[1]]
        elif op == "1RR":
            src = dst = at(mod4(u - 1), v, halves[0])
            dev = right1
        elif op == "1LL":
            src = dst = at(mod4(u + 1), v, halves[1])
            dev = left1
        elif op in ("2R", "2L", "2O"):
            src = dst = at(every, v)
            dev = {"R": right2, "L": left2, "O": device(u, mod4(v + 2))}[op[1]]
        elif op == "2RR":
            src = dst = at(pl.ds(0, 2), mod4(v - 1))
            dev = right2
        elif op == "2LL":
            src = dst = at(pl.ds(2, 2), mod4(v + 1))
            dev = left2
        else:
            step = {"a": -1, "b": 1, "c": 2}[op[1]]
            src = dst = at(mod4(u + step), v) if op[0] == "X" else at(every, mod4(v + step))
            dev = {"cfg": 1 - core}
        index = ITEMS.index(item) * len(OPS) + OPS.index(op)
        return pltpu.make_async_remote_copy(
            src_ref=src,
            dst_ref=dst,
            send_sem=send_sem.at[index],
            recv_sem=recv_sem.at[index],
            device_id=dev,
            device_id_type=MESH,
        )

    plane_log = []

    def both(act):
        for core in (0, 1):
            pl.when(c == core)(functools.partial(act, core))

    def serve(*steps):
        steps = [step for step in steps if step[0] not in SKIP]
        for item, _, after in steps:
            plane_log.extend((item, op) for op in after.split())

        def act(core):
            for item, op, after in steps:
                if op:
                    plane(item, op, core).wait_recv()
                for follow in after.split():
                    plane(item, follow, core).start()

        if steps:
            both(act)

    def out_first():
        serve(("out", None, "1R 1L 1O"))

    def out_second():
        loads["out"].wait()
        serve(("out", "1R", "Xa"), ("out", "1L", "Xb"), ("out", "1O", "2R 2L 2O Xc"))

    def out_third():
        serve(("out", "2R", "Ya"), ("out", "2L", "Yb"), ("out", "2O", "Yc"))

    def first(item):
        serve((item, None, "1R 1L"))

    def second(item):
        serve((item, "1R", "1RR Xa"), (item, "1L", "1LL Xb"))

    def third(item):
        loads[item].wait()
        serve((item, "1RR", ""), (item, "1LL", "2R 2L Xc"))

    def fourth(item):
        serve((item, "2R", "2RR Ya"), (item, "2L", "2LL Yb"))

    def fifth(item):
        serve((item, "2RR", ""), (item, "2LL", "Yc"))

    def take(item):
        if item in SKIP:
            return

        def act(core):
            for op in ("Xa", "Xb", "Xc", "Ya", "Yb", "Yc"):
                plane(item, op, 1 - core).wait_recv()

        both(act)

    def fold(op, core):
        u, v = (x, y) if core == 0 else (y, x)

        def mod4(i):
            return lax.rem(i + 4, 4)

        one = {"R": 1, "L": -1, "O": 2}[op[1]]
        side = "RLO".index(op[1])
        uu, vv = (mod4(u + one), v) if op[0] in "125" else (u, mod4(v + one))
        dev = {"seq": vv * 4 + uu if core == 0 else uu * 4 + vv}
        if op[0] == "1":
            src, dst = gpart.at[mod4(u + 2), pl.ds(2 * side, 2)], gin1.at[side]
        elif op[0] == "2":
            src, dst = gpart.at[mod4(u + one)], gin2.at[side]
        elif op[0] == "3":
            src, dst = gmid.at[mod4(v + one)], gin3.at[side]
        elif op[0] == "4":
            src = dst = gfull.at[u, v]
        else:
            src = gfull.at[u] if len(op) == 2 else gfull.at[mod4(u - one), pl.ds(2 * side, 2)]
            dst = src
        index = N_PLANE + N_RING + N_VEL + FOLD_OPS.index(op)
        return pltpu.make_async_remote_copy(
            src_ref=src,
            dst_ref=dst,
            send_sem=send_sem.at[index],
            recv_sem=recv_sem.at[index],
            device_id=dev,
            device_id_type=MESH,
        )

    fold_log = []

    def fold_step(*steps):
        if "fold" in SKIP:
            return
        for _, _, after in steps:
            fold_log.extend(after.split())

        def act(core):
            for op, add, after in steps:
                if op:
                    fold(op, core).wait_recv()
                if add:
                    add(core)
                for follow in after.split():
                    fold(follow, core).start()

        both(act)

    def across(core, step):
        u, v = (x, y) if core == 0 else (y, x)
        return lax.rem(u + step + 4, 4), lax.rem(v + step + 4, 4)

    def add1(side):
        def add(core):
            u = across(core, 1 - 2 * side)[0]
            for i in range(2):
                place = 2 * side + i
                total = gpart[u, place].astype(F32) + gin1[side, i].astype(F32)
                gpart[u, place] = total.astype(BF16)

        return add

    def add2(core):
        u = across(core, 0)[0]
        for i in range(4):
            total = gpart[u, i].astype(F32) + gin2[0, i].astype(F32) + gin2[1, i].astype(F32)
            gmid[i] = total.astype(BF16)

    def add3(core):
        u, v = across(core, 0)
        total = gmid[v].astype(F32)
        for side in range(3):
            total = total + gin3[side].astype(F32)
        gfull[u, v] = total.astype(BF16)

    def fold_local():
        if "fold" in SKIP:
            return
        window = pl.ds(pl.multiple_of((s // 2) * 384, 128), 384)
        odd = s % 2 == 1

        def mine(block):
            return jnp.where(odd, pltpu.roll(block, 192, 1), block)[:, 0:192]

        final = mine(wf[:, window].astype(F32))
        down_rows = down[...].reshape(192, 1536)
        for r in range(8):
            gate = mine(jnp.broadcast_to(mod[r, 3:4, window], (8, 384)))[0:1]
            product = nn_dot((final * gate).astype(BF16), down_rows)
            gpart[r // 2, 2 * (r % 2)] = product[0:32].astype(BF16)
            gpart[r // 2, 2 * (r % 2) + 1] = product[32:64].astype(BF16)

    def ring(which, chunk, op):
        k = int(op[1])
        right = op[0] == "R"
        owner = ring8(1 - k if right else k - 1)
        if which == 0:
            src = abuf.at[owner, :, pl.ds(768 * chunk, 768)]
        else:
            src = rbuf.at[owner, pl.ds(4 * chunk, 4)]
        index = N_PLANE + (which * 2 + chunk) * len(RING_OPS) + RING_OPS.index(op)
        return pltpu.make_async_remote_copy(
            src_ref=src,
            dst_ref=src,
            send_sem=send_sem.at[index],
            recv_sem=recv_sem.at[index],
            device_id={"req": ring8(1 if right else -1)},
            device_id_type=MESH,
        )

    def ring_go(which, chunk, *ops):
        for op in ops:
            if "ring%d" % which not in SKIP:
                ring(which, chunk, op).start()
                started.append(ring(which, chunk, op))

    def hop(which, chunk, k):
        if "ring%d" % which in SKIP:
            return
        for side in "RL":
            if k < 4 or chunk == "RL".index(side):
                ring(which, chunk, side + str(k)).wait_recv()
            if k < 3 or (k == 3 and chunk == "RL".index(side)):
                ring_go(which, chunk, side + str(k + 1))

    def fresh_copy(half, step):
        spot = fbuf.at[y, x, :, pl.ds(768 * half, 768)]
        index = N_COPY - 33 + 16 * half + step
        return pltpu.make_async_remote_copy(
            src_ref=spot,
            dst_ref=spot,
            send_sem=send_sem.at[index],
            recv_sem=recv_sem.at[index],
            device_id={"seq": lax.rem(y + step // 4, 4) * 4 + lax.rem(x + step % 4, 4)},
            device_id_type=MESH,
        )

    def fresh_go(half):
        if "fresh" not in SKIP:
            for step in (10, 9, 11, 6, 14, 5, 7, 13, 15, 2, 8, 1, 3, 4, 12):
                fresh_copy(half, step).start()
                started.append(fresh_copy(half, step))

    def fresh_wait(half):
        if "fresh" not in SKIP:
            for step in range(1, 16):
                fresh_copy(half, step).wait_recv()

    barrier = pltpu.get_barrier_semaphore()
    greeted = [{"cfg": 1 - c}]
    for step in range(1, 16):
        greeted.append({"seq": lax.rem(s + step, 16)})
    for step in range(1, 8):
        greeted.append({"req": ring8(step)})
    for device in greeted:
        pl.semaphore_signal(barrier, inc=1, device_id=device, device_id_type=MESH)

    lane = lax.broadcasted_iota(jnp.int32, (8, 128), 1)
    row = lax.broadcasted_iota(jnp.int32, (8, 128), 0)
    pair = lane // 2
    offset = jnp.where(pair < 8, 0, jnp.where(pair < 36, 8, 36))
    span = jnp.where(pair < 8, 16.0, 56.0)
    frequency = jnp.exp(-(2.0 * (pair - offset).astype(F32) / span) * math.log(10000.0))
    place = jnp.zeros((8, 128), F32)
    for j in range(6):
        ids = [jnp.full((8, 128), pos_ref[axis, 0, j], jnp.int32).astype(F32) for axis in range(3)]
        here = jnp.where(pair < 8, ids[0], jnp.where(pair < 36, ids[1], ids[2]))
        place = jnp.where(row == j, here, place)
    angle = place * frequency
    even = lax.rem(lane, 2) == 0
    cosine = jnp.cos(angle)
    sine = jnp.sin(angle)
    sine = jnp.where(even, -sine, sine)
    ftmp[...] = jnp.zeros_like(ftmp)
    for j in range(6):
        two = fresh_ref[j].astype(F32)
        ftmp[j : j + 1, :] = two[0:1]
        ftmp[8 + j : 9 + j, :] = two[1:2]
    for h in range(12):
        k = ftmp[0:8, h * 128 : (h + 1) * 128]
        swapped = jnp.where(even, pltpu.roll(k, 127, 1), pltpu.roll(k, 1, 1))
        turned = k * cosine + swapped * sine
        v = ftmp[8:16, h * 128 : (h + 1) * 128]
        fbuf[y, x, :, h * 128 : (h + 1) * 128] = jnp.concatenate([turned, v], axis=0).astype(BF16)

    pl.semaphore_wait(barrier, len(greeted))

    out_first()
    fresh_go(0)
    fresh_go(1)

    length = len_ref[z]
    key_place = lax.broadcasted_iota(jnp.int32, (8, 768), 1)
    new_place = lax.broadcasted_iota(jnp.int32, (8, 128), 1)

    def mark(k, carry):
        replaced, slots = carry
        for j in range(6):
            slot = slot_ref[0, k * 6 + j]
            replaced = jnp.where(key_place == slot, 1, replaced)
            slots = jnp.where(new_place == k * 8 + j, slot, slots)
        return replaced, slots

    replaced, slots = lax.fori_loop(
        0, 16, mark, (jnp.zeros((8, 768), jnp.int32), jnp.full((8, 128), -1, jnp.int32))
    )
    bias_img = jnp.where((key_place < length) & (replaced == 0), 0.0, NEG).astype(F32)[0:1]
    bias_new = jnp.where((slots >= 0) & (slots < length), 0.0, NEG).astype(F32)[0:1]

    def cached_heads(*heads):
        if "attn" in SKIP:
            return
        for h in heads:
            cols = pl.ds(h * 128, 128)
            q = q_ref[:, cols]
            st = nt_dot(q, text[0, :, cols]) * SCALE
            si = nt_dot(q, img[0, :, cols]) * SCALE + bias_img
            m = jnp.maximum(jnp.max(st, axis=-1, keepdims=True), jnp.max(si, axis=-1, keepdims=True))
            pt = jnp.exp(st - m)
            pi = jnp.exp(si - m)
            total = jnp.sum(pt, axis=-1, keepdims=True) + jnp.sum(pi, axis=-1, keepdims=True)
            o = nn_dot(pt.astype(BF16), text[1, :, cols]) + nn_dot(pi.astype(BF16), img[1, :, cols])
            att_o[h] = o
            att_m[h] = jnp.broadcast_to(m, (48, 128))
            att_l[h] = jnp.broadcast_to(total, (48, 128))

    def fresh_heads(*heads):
        if "attn" in SKIP:
            return
        for h in heads:
            cols = pl.ds(h * 128, 128)
            q = q_ref[:, cols]
            kv = fbuf[:, :, :, cols].astype(F32)
            kf = kv[:, :, :8].reshape(128, 128).astype(BF16)
            vf = kv[:, :, 8:].reshape(128, 128).astype(BF16)
            sf = nt_dot(q, kf) * SCALE + bias_new
            before = att_m[h][:, 0:1]
            m = jnp.maximum(before, jnp.max(sf, axis=-1, keepdims=True))
            pf = jnp.exp(sf - m)
            keep = jnp.exp(before - m)
            total = att_l[h][:, 0:1] * keep + jnp.sum(pf, axis=-1, keepdims=True)
            o = att_o[h] * keep + nn_dot(pf.astype(BF16), vf)
            abuf[z, :, cols] = (o / total).astype(BF16)

    def project(*steps):
        if "proj" in SKIP:
            return
        for step in steps:
            r = ring8(step)
            rows = nn_dot(abuf[r], obuf[...].reshape(1536, 384))
            gate = mod[r, 0:1, pl.ds(pl.multiple_of(z * 384, 128), 384)]
            rbuf[z, (step + 1) % 8] = (stream[r].astype(F32) + gate * rows).astype(BF16)

    def normalize(r, carry):
        parts = [rbuf[b, lax.rem(r - b + 9, 8)].astype(F32) for b in range(8)]
        row_sum = sum(jnp.sum(p, axis=-1, keepdims=True) for p in parts)
        average = row_sum * (1.0 / 3072.0)
        centered = [p - average for p in parts]
        spread = sum(jnp.sum(p * p, axis=-1, keepdims=True) for p in centered) * (1.0 / 3072.0)
        inverse = lax.rsqrt(spread + EPSILON)
        for b in range(8):
            cols = pl.ds(b * 384, 384)
            gain = 1.0 + mod[r, 2:3, cols]
            shift = mod[r, 1:2, cols]
            nbuf[r, :, cols] = (centered[b] * inverse * gain + shift).astype(BF16)
        return carry

    def up_half(half):
        def tile(t, carry):
            cols = pl.ds(pl.multiple_of(t * 256, 256), 256)
            weights = ubuf[half, :, :, :, :, cols].reshape(3072, 256)
            pre = nn_dot(nbuf[...].reshape(384, 3072), weights)
            actbuf[half, :, cols] = jax.nn.gelu(pre, approximate=True).astype(BF16)
            return carry

        if "mm" not in SKIP:
            lax.fori_loop(0, 3, tile, 0)

    def velocity(r, carry):
        fold_r = gfull[lax.div(r, 2), pl.ds(2 * lax.rem(r, 2), 2)].reshape(64, 1536)
        rows = nt_dot(actbuf[0, pl.ds(r * 48, 48)], fold_r[:, 0:768])
        rows += nt_dot(actbuf[1, pl.ds(r * 48, 48)], fold_r[:, 768:1536])
        vel[r, :, 0:64] += rows
        return carry

    for name in ("mod", "wf", "down"):
        loads[name].wait()
    fold_local()
    for name in ("q", "tk", "ik", "tv", "iv"):
        loads[name].wait()
    cached_heads(0, 1, 2, 3)
    first("up0")
    first("up1")
    cached_heads(4, 5, 6, 7)
    out_second()
    cached_heads(8, 9, 10, 11)
    fresh_wait(0)
    fresh_heads(0, 1, 2, 3, 4, 5)
    ring_go(0, 0, "R1", "L1")
    second("up0")
    second("up1")
    fresh_wait(1)
    fresh_heads(6, 7, 8, 9, 10, 11)
    ring_go(0, 1, "R1", "L1")
    fold_step((None, None, "1R 1L"))
    out_third()
    third("up0")
    hop(0, 0, 1)
    hop(0, 1, 1)
    third("up1")
    fold_step(("1R", add1(0), "2R"), ("1L", add1(1), "2L"))
    loads["stream"].wait()
    take("out")
    project(0)
    hop(0, 0, 2)
    hop(0, 1, 2)
    project(-1, 1, 2)
    ring_go(1, 0, "R1", "L1")
    hop(0, 0, 3)
    hop(0, 1, 3)
    project(-2, 3, -3)
    hop(0, 0, 4)
    hop(0, 1, 4)
    project(4)
    ring_go(1, 1, "R1", "L1")
    fold_step(("2R", None, ""), ("2L", add2, "3R 3L 3O"))
    fourth("up0")
    hop(1, 0, 1)
    fold_step(("3R", None, ""), ("3L", None, ""), ("3O", add3, "4R 4L 4O"))
    hop(1, 1, 1)
    hop(1, 0, 2)
    fold_step(("4R", None, ""), ("4L", None, ""), ("4O", None, "5R 5L"))
    hop(1, 1, 2)
    fourth("up1")
    fifth("up0")
    hop(1, 0, 3)
    hop(1, 1, 3)
    fold_step(("5R", None, "5RR"), ("5L", None, "5LL"))
    fifth("up1")
    vel[...] = jnp.zeros_like(vel)
    hop(1, 0, 4)
    hop(1, 1, 4)
    if "norm" not in SKIP:
        lax.fori_loop(0, 8, normalize, 0)
    own = jnp.concatenate([rbuf[b, lax.rem(z - b + 9, 8)] for b in range(8)], axis=-1)
    vel[z, :, 0:64] = nt_dot(own, wf[...])
    take("up0")
    up_half(0)
    take("up1")
    up_half(1)
    fold_step(("5RR", None, ""), ("5LL", None, ""))
    if "mm" not in SKIP:
        lax.fori_loop(0, 8, velocity, 0)

    even_core = c == 0
    scale = jnp.where(even_core, GUIDANCE, 1.0 - GUIDANCE)
    for r in range(8):
        evens = vel[r, pl.ds(0, 24, stride=2), :] * scale
        odds = vel[r, pl.ds(1, 24, stride=2), :] * scale
        part[r] = jnp.where(even_core, evens, odds)
        swap_out[r] = jnp.where(even_core, odds, evens)
    swap = pltpu.make_async_remote_copy(
        src_ref=swap_out,
        dst_ref=swap_in,
        send_sem=send_sem.at[N_COPY - 1],
        recv_sem=recv_sem.at[N_COPY - 1],
        device_id={"cfg": 1 - c},
        device_id_type=MESH,
    )
    swap.start()
    started.append(swap)
    swap.wait_recv()
    part[...] = part[...] + swap_in[...]

    def velocity_copy(step):
        target = ring8(step)
        index = N_PLANE + N_RING + step
        return pltpu.make_async_remote_copy(
            src_ref=part.at[target],
            dst_ref=partin.at[step],
            send_sem=send_sem.at[index],
            recv_sem=recv_sem.at[index],
            device_id={"req": target},
            device_id_type=MESH,
        )

    for step in (4, 3, 5, 2, 6, 1, 7):
        velocity_copy(step).start()
        started.append(velocity_copy(step))
    index = jnp.full((24, 64), step_ref[0], jnp.int32)
    now = noise_level(index)
    later = noise_level(index + 1)
    token = s * 48 + 2 * lax.broadcasted_iota(jnp.int32, (24, 64), 0) + c
    valid = token < length
    current = lat_ref[...]
    guided = part[z]
    for step in range(1, 8):
        velocity_copy(step).wait_recv()
        guided = guided + partin[step]
    guided = guided[:, 0:64]
    res_ref[0] = jnp.where(valid, current + (later - now) * guided, current)
    res_ref[1] = jnp.where(valid, current - now * guided, current)

    def finish(core):
        for item, op in plane_log:
            plane(item, op, core).wait_send()
        for op in fold_log:
            fold(op, core).wait_send()

    both(finish)
    for copy in started:
        copy.wait_send()


def per_device(
    queries,
    text_cache,
    image_cache,
    fresh_kv,
    fresh_slots,
    fresh_pos,
    image_len,
    stream,
    modulation,
    out_weight,
    up_weight,
    down_weight,
    final_weight,
    latent,
    step_index,
):
    vmem = pl.BlockSpec(memory_space=pltpu.VMEM)
    smem = pl.BlockSpec(memory_space=pltpu.SMEM)
    hbm = pl.BlockSpec(memory_space=pl.ANY)
    both = pl.pallas_call(
        kernel,
        out_shape=jax.ShapeDtypeStruct((2, 24, 64), F32),
        in_specs=[smem] * 4 + [hbm] * 3 + [vmem] + [hbm] * 6 + [vmem],
        out_specs=vmem,
        scratch_shapes=[
            pltpu.VMEM((48, 1536), BF16),
            pltpu.VMEM((2, 512, 1536), BF16),
            pltpu.VMEM((2, 768, 1536), BF16),
            pltpu.VMEM((8, 48, 384), BF16),
            pltpu.VMEM((8, 4, 3072), F32),
            pltpu.VMEM((64, 3072), BF16),
            pltpu.VMEM((16, 1536), F32),
            pltpu.VMEM((4, 4, 16, 1536), BF16),
            pltpu.VMEM((4, 4, 2, 48, 384), BF16),
            pltpu.VMEM((2, 4, 4, 2, 96, 768), BF16),
            pltpu.VMEM((2, 96, 1536), BF16),
            pltpu.VMEM((4, 4, 32, 1536), BF16),
            pltpu.VMEM((4, 32, 1536), BF16),
            pltpu.VMEM((4, 4, 32, 1536), BF16),
            pltpu.VMEM((2, 2, 32, 1536), BF16),
            pltpu.VMEM((2, 4, 32, 1536), BF16),
            pltpu.VMEM((3, 32, 1536), BF16),
            pltpu.VMEM((8, 48, 1536), BF16),
            pltpu.VMEM((8, 8, 48, 384), BF16),
            pltpu.VMEM((8, 48, 3072), BF16),
            pltpu.VMEM((2, 384, 768), BF16),
            pltpu.VMEM((12, 48, 128), F32),
            pltpu.VMEM((12, 48, 128), F32),
            pltpu.VMEM((12, 48, 128), F32),
            pltpu.VMEM((8, 48, 128), F32),
            pltpu.VMEM((8, 24, 128), F32),
            pltpu.VMEM((8, 24, 128), F32),
            pltpu.VMEM((8, 24, 128), F32),
            pltpu.VMEM((8, 24, 128), F32),
            pltpu.SemaphoreType.DMA((12,)),
            pltpu.SemaphoreType.DMA((N_COPY,)),
            pltpu.SemaphoreType.DMA((N_COPY,)),
        ],
        compiler_params=pltpu.CompilerParams(
            collective_id=0, has_side_effects=True, vmem_limit_bytes=60 * 1024 * 1024
        ),
    )(
        image_len,
        step_index,
        fresh_slots,
        fresh_pos,
        queries[0, 0],
        text_cache[0, 0],
        image_cache[0, 0],
        fresh_kv[0, 0].transpose(1, 0, 2),
        stream[0],
        modulation,
        out_weight.reshape(2, 48, 384),
        up_weight.reshape(2, 96, 1536),
        down_weight.T.reshape(2, 96, 1536),
        final_weight.T,
        latent[0],
    )
    return (both[0][None], both[1][None])


def solution(mesh):
    in_specs = (
        P("cfg", "req", "seq", None),
        P("cfg", "req", None, None, None),
        P("cfg", "req", None, None, None),
        P("cfg", "req", None, "seq", None),
        P("req", None),
        P(None, "req", "seq"),
        P(),
        P("cfg", None, "seq", "req"),
        P(),
        P("seq", "req"),
        P("seq", "req"),
        P("req", "seq"),
        P(),
        P("req", "seq", "cfg"),
        P(),
    )
    out_specs = (P("req", "seq", "cfg"), P("req", "seq", "cfg"))
    return jax.shard_map(
        per_device, mesh=mesh, in_specs=in_specs, out_specs=out_specs, check_vma=False
    )
```

```python
import functools
import math

import jax
import jax.numpy as jnp
from jax import lax
from jax.experimental import pallas as pl
from jax.experimental.pallas import tpu as pltpu
from jax.sharding import PartitionSpec as P

STEPS = 28
GUIDANCE = 3.0
SHIFT = 3.0
SCALE = 1.0 / math.sqrt(128.0)
EPSILON = 1e-06
MESH = pl.DeviceIdType.MESH
F32 = jnp.float32
BF16 = jnp.bfloat16
NEG = -jnp.inf
SKIP = frozenset()

ITEMS = ("out", "up0", "up1")
OPS = ("1R", "1L", "1O", "2O", "1RR", "1LL", "2R", "2L", "2RR", "2LL", "Xa", "Xb", "Xc", "Ya", "Yb", "Yc")
N_PLANE = len(ITEMS) * len(OPS)
RING_OPS = ("R1", "R2", "R3", "R4", "L1", "L2", "L3", "L4")
N_RING = 4 * len(RING_OPS)
N_VEL = 8
FOLD_OPS = ("1R", "1L", "2R", "2L", "3R", "3L", "3O", "4R", "4L", "4O", "5R", "5L", "5RR", "5LL")
N_FOLD = len(FOLD_OPS)
N_COPY = N_PLANE + N_RING + N_VEL + N_FOLD + 32 + 1


def nt_dot(a, b):
    return lax.dot_general(a, b, (((1,), (1,)), ((), ())), preferred_element_type=F32)


def nn_dot(a, b):
    return jnp.dot(a, b, preferred_element_type=F32)


def noise_level(index):
    fraction = 1.0 - index.astype(F32) / STEPS
    return SHIFT * fraction / (SHIFT * fraction + 1.0 - fraction)


def kernel(
    len_ref,
    step_ref,
    slot_ref,
    pos_ref,
    q_hbm,
    text_hbm,
    img_hbm,
    fresh_ref,
    stream_hbm,
    mod_hbm,
    out_hbm,
    up_hbm,
    down_hbm,
    wf_hbm,
    lat_ref,
    res_ref,
    q_ref,
    text,
    img,
    stream,
    mod,
    wf,
    ftmp,
    fbuf,
    obuf,
    ubuf,
    down,
    gpart,
    gmid,
    gfull,
    gin1,
    gin2,
    gin3,
    abuf,
    rbuf,
    nbuf,
    actbuf,
    att_o,
    att_m,
    att_l,
    vel,
    swap_out,
    swap_in,
    part,
    partin,
    load_sem,
    send_sem,
    recv_sem,
):
    c = lax.axis_index("cfg")
    z = lax.axis_index("req")
    s = lax.axis_index("seq")
    y = s // 4
    x = s % 4

    def ring8(i):
        return lax.rem(z + i + 8, 8)

    started = []

    loads = {}

    def load(name, src, dst):
        loads[name] = pltpu.make_async_copy(src, dst, load_sem.at[len(loads)])
        loads[name].start()

    load("mod", mod_hbm.at[c], mod)
    load("wf", wf_hbm, wf)
    load("down", down_hbm, down)
    load("q", q_hbm, q_ref)
    load("tk", text_hbm.at[0], text.at[0])
    load("ik", img_hbm.at[0], img.at[0])
    load("tv", text_hbm.at[1], text.at[1])
    load("iv", img_hbm.at[1], img.at[1])
    load("out", out_hbm, obuf.at[y, x])
    for half in (0, 1):
        load("up%d" % half, up_hbm.at[:, :, pl.ds(768 * half, 768)], ubuf.at[half, y, x])
    load("stream", stream_hbm, stream)

    def plane(item, op, core):
        half = int(item[-1]) if item[-1] in "01" else 0
        if item == "out":
            buf, shard = obuf, out_hbm.at[core]
        else:
            buf, shard = ubuf.at[half], up_hbm.at[core, :, pl.ds(768 * half, 768)]
        u, v = (x, y) if core == 0 else (y, x)
        def mod4(i):
            return lax.rem(i + 4, 4)

        def at(uu, vv, extra=()):
            where = (vv, uu) if core == 0 else (uu, vv)
            return buf.at[where + (core,) + extra]

        def device(uu, vv):
            return {"seq": vv * 4 + uu if core == 0 else uu * 4 + vv}

        if item == "out":
            halves = ((pl.ds(0, 32),), (pl.ds(32, 16),))
        else:
            halves = ((pl.ds(0, 48),), (pl.ds(48, 48),))
        right1, left1 = device(mod4(u + 1), v), device(mod4(u - 1), v)
        right2, left2 = device(u, mod4(v + 1)), device(u, mod4(v - 1))
        every = slice(None)
        if op in ("1R", "1L", "1O"):
            src, dst = shard, at(u, v)
            dev = {"R": right1, "L": left1, "O": device(mod4(u + 2), v)}[op[1]]
        elif op == "1RR":
            src = dst = at(mod4(u - 1), v, halves[0])
            dev = right1
        elif op == "1LL":
            src = dst = at(mod4(u + 1), v, halves[1])
            dev = left1
        elif op in ("2R", "2L", "2O"):
            src = dst = at(every, v)
            dev = {"R": right2, "L": left2, "O": device(u, mod4(v + 2))}[op[1]]
        elif op == "2RR":
            src = dst = at(pl.ds(0, 2), mod4(v - 1))
            dev = right2
        elif op == "2LL":
            src = dst = at(pl.ds(2, 2), mod4(v + 1))
            dev = left2
        else:
            step = {"a": -1, "b": 1, "c": 2}[op[1]]
            src = dst = at(mod4(u + step), v) if op[0] == "X" else at(every, mod4(v + step))
            dev = {"cfg": 1 - core}
        index = ITEMS.index(item) * len(OPS) + OPS.index(op)
        return pltpu.make_async_remote_copy(
            src_ref=src,
            dst_ref=dst,
            send_sem=send_sem.at[index],
            recv_sem=recv_sem.at[index],
            device_id=dev,
            device_id_type=MESH,
        )

    plane_log = []

    def both(act):
        for core in (0, 1):
            pl.when(c == core)(functools.partial(act, core))

    def serve(*steps):
        steps = [step for step in steps if step[0] not in SKIP]
        for item, _, after in steps:
            plane_log.extend((item, op) for op in after.split())

        def act(core):
            for item, op, after in steps:
                if op:
                    plane(item, op, core).wait_recv()
                for follow in after.split():
                    plane(item, follow, core).start()

        if steps:
            both(act)

    def out_first():
        serve(("out", None, "1R 1L 1O"))

    def out_second():
        loads["out"].wait()
        serve(("out", "1R", "Xa"), ("out", "1L", "Xb"), ("out", "1O", "2R 2L 2O Xc"))

    def out_third():
        serve(("out", "2R", "Ya"), ("out", "2L", "Yb"), ("out", "2O", "Yc"))

    def first(item):
        serve((item, None, "1R 1L"))

    def second(item):
        serve((item, "1R", "1RR Xa"), (item, "1L", "1LL Xb"))

    def third(item):
        loads[item].wait()
        serve((item, "1RR", ""), (item, "1LL", "2R 2L Xc"))

    def fourth(item):
        serve((item, "2R", "2RR Ya"), (item, "2L", "2LL Yb"))

    def fifth(item):
        serve((item, "2RR", ""), (item, "2LL", "Yc"))

    def take(item):
        if item in SKIP:
            return

        def act(core):
            for op in ("Xa", "Xb", "Xc", "Ya", "Yb", "Yc"):
                plane(item, op, 1 - core).wait_recv()

        both(act)

    def fold(op, core):
        u, v = (x, y) if core == 0 else (y, x)

        def mod4(i):
            return lax.rem(i + 4, 4)

        one = {"R": 1, "L": -1, "O": 2}[op[1]]
        side = "RLO".index(op[1])
        uu, vv = (mod4(u + one), v) if op[0] in "125" else (u, mod4(v + one))
        dev = {"seq": vv * 4 + uu if core == 0 else uu * 4 + vv}
        if op[0] == "1":
            src, dst = gpart.at[mod4(u + 2), pl.ds(2 * side, 2)], gin1.at[side]
        elif op[0] == "2":
            src, dst = gpart.at[mod4(u + one)], gin2.at[side]
        elif op[0] == "3":
            src, dst = gmid.at[mod4(v + one)], gin3.at[side]
        elif op[0] == "4":
            src = dst = gfull.at[u, v]
        else:
            src = gfull.at[u] if len(op) == 2 else gfull.at[mod4(u - one), pl.ds(2 * side, 2)]
            dst = src
        index = N_PLANE + N_RING + N_VEL + FOLD_OPS.index(op)
        return pltpu.make_async_remote_copy(
            src_ref=src,
            dst_ref=dst,
            send_sem=send_sem.at[index],
            recv_sem=recv_sem.at[index],
            device_id=dev,
            device_id_type=MESH,
        )

    fold_log = []

    def fold_step(*steps):
        if "fold" in SKIP:
            return
        for _, _, after in steps:
            fold_log.extend(after.split())

        def act(core):
            for op, add, after in steps:
                if op:
                    fold(op, core).wait_recv()
                if add:
                    add(core)
                for follow in after.split():
                    fold(follow, core).start()

        both(act)

    def across(core, step):
        u, v = (x, y) if core == 0 else (y, x)
        return lax.rem(u + step + 4, 4), lax.rem(v + step + 4, 4)

    def add1(side):
        def add(core):
            u = across(core, 1 - 2 * side)[0]
            for i in range(2):
                place = 2 * side + i
                total = gpart[u, place].astype(F32) + gin1[side, i].astype(F32)
                gpart[u, place] = total.astype(BF16)

        return add

    def add2(core):
        u = across(core, 0)[0]
        for i in range(4):
            total = gpart[u, i].astype(F32) + gin2[0, i].astype(F32) + gin2[1, i].astype(F32)
            gmid[i] = total.astype(BF16)

    def add3(core):
        u, v = across(core, 0)
        total = gmid[v].astype(F32)
        for side in range(3):
            total = total + gin3[side].astype(F32)
        gfull[u, v] = total.astype(BF16)

    def fold_local():
        if "fold" in SKIP:
            return
        window = pl.ds(pl.multiple_of((s // 2) * 384, 128), 384)
        odd = s % 2 == 1

        def mine(block):
            return jnp.where(odd, pltpu.roll(block, 192, 1), block)[:, 0:192]

        final = mine(wf[:, window].astype(F32))
        down_rows = down[...].reshape(192, 1536)
        for r in range(8):
            gate = mine(jnp.broadcast_to(mod[r, 3:4, window], (8, 384)))[0:1]
            product = nn_dot((final * gate).astype(BF16), down_rows)
            gpart[r // 2, 2 * (r % 2)] = product[0:32].astype(BF16)
            gpart[r // 2, 2 * (r % 2) + 1] = product[32:64].astype(BF16)

    def ring(which, chunk, op):
        k = int(op[1])
        right = op[0] == "R"
        owner = ring8(1 - k if right else k - 1)
        if which == 0:
            src = abuf.at[owner, :, pl.ds(768 * chunk, 768)]
        else:
            src = rbuf.at[owner, pl.ds(4 * chunk, 4)]
        index = N_PLANE + (which * 2 + chunk) * len(RING_OPS) + RING_OPS.index(op)
        return pltpu.make_async_remote_copy(
            src_ref=src,
            dst_ref=src,
            send_sem=send_sem.at[index],
            recv_sem=recv_sem.at[index],
            device_id={"req": ring8(1 if right else -1)},
            device_id_type=MESH,
        )

    def ring_go(which, chunk, *ops):
        for op in ops:
            if "ring%d" % which not in SKIP:
                ring(which, chunk, op).start()
                started.append(ring(which, chunk, op))

    def hop(which, chunk, k):
        if "ring%d" % which in SKIP:
            return
        for side in "RL":
            if k < 4 or chunk == "RL".index(side):
                ring(which, chunk, side + str(k)).wait_recv()
            if k < 3 or (k == 3 and chunk == "RL".index(side)):
                ring_go(which, chunk, side + str(k + 1))

    def fresh_copy(half, step):
        spot = fbuf.at[y, x, :, pl.ds(768 * half, 768)]
        index = N_COPY - 33 + 16 * half + step
        return pltpu.make_async_remote_copy(
            src_ref=spot,
            dst_ref=spot,
            send_sem=send_sem.at[index],
            recv_sem=recv_sem.at[index],
            device_id={"seq": lax.rem(y + step // 4, 4) * 4 + lax.rem(x + step % 4, 4)},
            device_id_type=MESH,
        )

    def fresh_go(half):
        if "fresh" not in SKIP:
            for step in (10, 9, 11, 6, 14, 5, 7, 13, 15, 2, 8, 1, 3, 4, 12):
                fresh_copy(half, step).start()
                started.append(fresh_copy(half, step))

    def fresh_wait(half):
        if "fresh" not in SKIP:
            for step in range(1, 16):
                fresh_copy(half, step).wait_recv()

    barrier = pltpu.get_barrier_semaphore()
    greeted = [{"cfg": 1 - c}]
    for step in range(1, 16):
        greeted.append({"seq": lax.rem(s + step, 16)})
    for step in range(1, 8):
        greeted.append({"req": ring8(step)})
    for device in greeted:
        pl.semaphore_signal(barrier, inc=1, device_id=device, device_id_type=MESH)

    lane = lax.broadcasted_iota(jnp.int32, (8, 128), 1)
    row = lax.broadcasted_iota(jnp.int32, (8, 128), 0)
    pair = lane // 2
    offset = jnp.where(pair < 8, 0, jnp.where(pair < 36, 8, 36))
    span = jnp.where(pair < 8, 16.0, 56.0)
    frequency = jnp.exp(-(2.0 * (pair - offset).astype(F32) / span) * math.log(10000.0))
    place = jnp.zeros((8, 128), F32)
    for j in range(6):
        ids = [jnp.full((8, 128), pos_ref[axis, 0, j], jnp.int32).astype(F32) for axis in range(3)]
        here = jnp.where(pair < 8, ids[0], jnp.where(pair < 36, ids[1], ids[2]))
        place = jnp.where(row == j, here, place)
    angle = place * frequency
    even = lax.rem(lane, 2) == 0
    cosine = jnp.cos(angle)
    sine = jnp.sin(angle)
    sine = jnp.where(even, -sine, sine)
    ftmp[...] = jnp.zeros_like(ftmp)
    for j in range(6):
        two = fresh_ref[j].astype(F32)
        ftmp[j : j + 1, :] = two[0:1]
        ftmp[8 + j : 9 + j, :] = two[1:2]
    for h in range(12):
        k = ftmp[0:8, h * 128 : (h + 1) * 128]
        swapped = jnp.where(even, pltpu.roll(k, 127, 1), pltpu.roll(k, 1, 1))
        turned = k * cosine + swapped * sine
        v = ftmp[8:16, h * 128 : (h + 1) * 128]
        fbuf[y, x, :, h * 128 : (h + 1) * 128] = jnp.concatenate([turned, v], axis=0).astype(BF16)

    pl.semaphore_wait(barrier, len(greeted))

    out_first()
    fresh_go(0)
    fresh_go(1)

    length = len_ref[z]
    key_place = lax.broadcasted_iota(jnp.int32, (8, 768), 1)
    new_place = lax.broadcasted_iota(jnp.int32, (8, 128), 1)

    def mark(k, carry):
        replaced, slots = carry
        for j in range(6):
            slot = slot_ref[0, k * 6 + j]
            replaced = jnp.where(key_place == slot, 1, replaced)
            slots = jnp.where(new_place == k * 8 + j, slot, slots)
        return replaced, slots

    replaced, slots = lax.fori_loop(
        0, 16, mark, (jnp.zeros((8, 768), jnp.int32), jnp.full((8, 128), -1, jnp.int32))
    )
    bias_img = jnp.where((key_place < length) & (replaced == 0), 0.0, NEG).astype(F32)[0:1]
    bias_new = jnp.where((slots >= 0) & (slots < length), 0.0, NEG).astype(F32)[0:1]

    def cached_heads(*heads):
        if "attn" in SKIP:
            return
        for h in heads:
            cols = pl.ds(h * 128, 128)
            q = q_ref[:, cols]
            st = nt_dot(q, text[0, :, cols]) * SCALE
            si = nt_dot(q, img[0, :, cols]) * SCALE + bias_img
            m = jnp.maximum(jnp.max(st, axis=-1, keepdims=True), jnp.max(si, axis=-1, keepdims=True))
            pt = jnp.exp(st - m)
            pi = jnp.exp(si - m)
            total = jnp.sum(pt, axis=-1, keepdims=True) + jnp.sum(pi, axis=-1, keepdims=True)
            o = nn_dot(pt.astype(BF16), text[1, :, cols]) + nn_dot(pi.astype(BF16), img[1, :, cols])
            att_o[h] = o
            att_m[h] = jnp.broadcast_to(m, (48, 128))
            att_l[h] = jnp.broadcast_to(total, (48, 128))

    def fresh_heads(*heads):
        if "attn" in SKIP:
            return
        for h in heads:
            cols = pl.ds(h * 128, 128)
            q = q_ref[:, cols]
            kv = fbuf[:, :, :, cols].astype(F32)
            kf = kv[:, :, :8].reshape(128, 128).astype(BF16)
            vf = kv[:, :, 8:].reshape(128, 128).astype(BF16)
            sf = nt_dot(q, kf) * SCALE + bias_new
            before = att_m[h][:, 0:1]
            m = jnp.maximum(before, jnp.max(sf, axis=-1, keepdims=True))
            pf = jnp.exp(sf - m)
            keep = jnp.exp(before - m)
            total = att_l[h][:, 0:1] * keep + jnp.sum(pf, axis=-1, keepdims=True)
            o = att_o[h] * keep + nn_dot(pf.astype(BF16), vf)
            abuf[z, :, cols] = (o / total).astype(BF16)

    def project(*steps):
        if "proj" in SKIP:
            return
        for step in steps:
            r = ring8(step)
            rows = nn_dot(abuf[r], obuf[...].reshape(1536, 384))
            gate = mod[r, 0:1, pl.ds(pl.multiple_of(z * 384, 128), 384)]
            rbuf[z, (step + 1) % 8] = (stream[r].astype(F32) + gate * rows).astype(BF16)

    def normalize(r, carry):
        parts = [rbuf[b, lax.rem(r - b + 9, 8)].astype(F32) for b in range(8)]
        row_sum = sum(jnp.sum(p, axis=-1, keepdims=True) for p in parts)
        average = row_sum * (1.0 / 3072.0)
        centered = [p - average for p in parts]
        spread = sum(jnp.sum(p * p, axis=-1, keepdims=True) for p in centered) * (1.0 / 3072.0)
        inverse = lax.rsqrt(spread + EPSILON)
        for b in range(8):
            cols = pl.ds(b * 384, 384)
            gain = 1.0 + mod[r, 2:3, cols]
            shift = mod[r, 1:2, cols]
            nbuf[r, :, cols] = (centered[b] * inverse * gain + shift).astype(BF16)
        return carry

    def up_half(half):
        def tile(t, carry):
            cols = pl.ds(pl.multiple_of(t * 256, 256), 256)
            weights = ubuf[half, :, :, :, :, cols].reshape(3072, 256)
            pre = nn_dot(nbuf[...].reshape(384, 3072), weights)
            actbuf[half, :, cols] = jax.nn.gelu(pre, approximate=True).astype(BF16)
            return carry

        if "mm" not in SKIP:
            lax.fori_loop(0, 3, tile, 0)

    def velocity(r, carry):
        fold_r = gfull[lax.div(r, 2), pl.ds(2 * lax.rem(r, 2), 2)].reshape(64, 1536)
        rows = nt_dot(actbuf[0, pl.ds(r * 48, 48)], fold_r[:, 0:768])
        rows += nt_dot(actbuf[1, pl.ds(r * 48, 48)], fold_r[:, 768:1536])
        vel[r, :, 0:64] += rows
        return carry

    for name in ("mod", "wf", "down"):
        loads[name].wait()
    fold_local()
    for name in ("q", "tk", "ik", "tv", "iv"):
        loads[name].wait()
    cached_heads(0, 1, 2, 3)
    first("up0")
    first("up1")
    cached_heads(4, 5, 6, 7)
    out_second()
    cached_heads(8, 9, 10, 11)
    fresh_wait(0)
    fresh_heads(0, 1, 2, 3, 4, 5)
    ring_go(0, 0, "R1", "L1")
    fresh_wait(1)
    fresh_heads(6, 7, 8, 9, 10, 11)
    ring_go(0, 1, "R1", "L1")
    fold_step((None, None, "1R 1L"))
    second("up0")
    second("up1")
    out_third()
    third("up0")
    hop(0, 0, 1)
    hop(0, 1, 1)
    third("up1")
    fold_step(("1R", add1(0), "2R"), ("1L", add1(1), "2L"))
    loads["stream"].wait()
    take("out")
    project(0)
    hop(0, 0, 2)
    hop(0, 1, 2)
    project(-1, 1, 2)
    ring_go(1, 0, "R1", "L1")
    hop(0, 0, 3)
    hop(0, 1, 3)
    project(-2, 3, -3)
    hop(0, 0, 4)
    hop(0, 1, 4)
    project(4)
    ring_go(1, 1, "R1", "L1")
    fold_step(("2R", None, ""), ("2L", add2, "3R 3L 3O"))
    hop(1, 0, 1)
    fourth("up0")
    fold_step(("3R", None, ""), ("3L", None, ""), ("3O", add3, "4R 4L 4O"))
    hop(1, 1, 1)
    hop(1, 0, 2)
    fold_step(("4R", None, ""), ("4L", None, ""), ("4O", None, "5R 5L"))
    hop(1, 1, 2)
    fourth("up1")
    fifth("up0")
    hop(1, 0, 3)
    hop(1, 1, 3)
    fold_step(("5R", None, "5RR"), ("5L", None, "5LL"))
    fifth("up1")
    vel[...] = jnp.zeros_like(vel)
    hop(1, 0, 4)
    hop(1, 1, 4)
    if "norm" not in SKIP:
        lax.fori_loop(0, 8, normalize, 0)
    own = jnp.concatenate([rbuf[b, lax.rem(z - b + 9, 8)] for b in range(8)], axis=-1)
    vel[z, :, 0:64] = nt_dot(own, wf[...])
    take("up0")
    up_half(0)
    take("up1")
    up_half(1)
    fold_step(("5RR", None, ""), ("5LL", None, ""))
    if "mm" not in SKIP:
        lax.fori_loop(0, 8, velocity, 0)

    even_core = c == 0
    scale = jnp.where(even_core, GUIDANCE, 1.0 - GUIDANCE)
    for r in range(8):
        evens = vel[r, pl.ds(0, 24, stride=2), :] * scale
        odds = vel[r, pl.ds(1, 24, stride=2), :] * scale
        part[r] = jnp.where(even_core, evens, odds)
        swap_out[r] = jnp.where(even_core, odds, evens)
    swap = pltpu.make_async_remote_copy(
        src_ref=swap_out,
        dst_ref=swap_in,
        send_sem=send_sem.at[N_COPY - 1],
        recv_sem=recv_sem.at[N_COPY - 1],
        device_id={"cfg": 1 - c},
        device_id_type=MESH,
    )
    swap.start()
    started.append(swap)
    swap.wait_recv()
    part[...] = part[...] + swap_in[...]

    def velocity_copy(step):
        target = ring8(step)
        index = N_PLANE + N_RING + step
        return pltpu.make_async_remote_copy(
            src_ref=part.at[target],
            dst_ref=partin.at[step],
            send_sem=send_sem.at[index],
            recv_sem=recv_sem.at[index],
            device_id={"req": target},
            device_id_type=MESH,
        )

    for step in (4, 3, 5, 2, 6, 1, 7):
        velocity_copy(step).start()
        started.append(velocity_copy(step))
    index = jnp.full((24, 64), step_ref[0], jnp.int32)
    now = noise_level(index)
    later = noise_level(index + 1)
    token = s * 48 + 2 * lax.broadcasted_iota(jnp.int32, (24, 64), 0) + c
    valid = token < length
    current = lat_ref[...]
    guided = part[z]
    for step in range(1, 8):
        velocity_copy(step).wait_recv()
        guided = guided + partin[step]
    guided = guided[:, 0:64]
    res_ref[0] = jnp.where(valid, current + (later - now) * guided, current)
    res_ref[1] = jnp.where(valid, current - now * guided, current)

    def finish(core):
        for item, op in plane_log:
            plane(item, op, core).wait_send()
        for op in fold_log:
            fold(op, core).wait_send()

    both(finish)
    for copy in started:
        copy.wait_send()


def per_device(
    queries,
    text_cache,
    image_cache,
    fresh_kv,
    fresh_slots,
    fresh_pos,
    image_len,
    stream,
    modulation,
    out_weight,
    up_weight,
    down_weight,
    final_weight,
    latent,
    step_index,
):
    vmem = pl.BlockSpec(memory_space=pltpu.VMEM)
    smem = pl.BlockSpec(memory_space=pltpu.SMEM)
    hbm = pl.BlockSpec(memory_space=pl.ANY)
    both = pl.pallas_call(
        kernel,
        out_shape=jax.ShapeDtypeStruct((2, 24, 64), F32),
        in_specs=[smem] * 4 + [hbm] * 3 + [vmem] + [hbm] * 6 + [vmem],
        out_specs=vmem,
        scratch_shapes=[
            pltpu.VMEM((48, 1536), BF16),
            pltpu.VMEM((2, 512, 1536), BF16),
            pltpu.VMEM((2, 768, 1536), BF16),
            pltpu.VMEM((8, 48, 384), BF16),
            pltpu.VMEM((8, 4, 3072), F32),
            pltpu.VMEM((64, 3072), BF16),
            pltpu.VMEM((16, 1536), F32),
            pltpu.VMEM((4, 4, 16, 1536), BF16),
            pltpu.VMEM((4, 4, 2, 48, 384), BF16),
            pltpu.VMEM((2, 4, 4, 2, 96, 768), BF16),
            pltpu.VMEM((2, 96, 1536), BF16),
            pltpu.VMEM((4, 4, 32, 1536), BF16),
            pltpu.VMEM((4, 32, 1536), BF16),
            pltpu.VMEM((4, 4, 32, 1536), BF16),
            pltpu.VMEM((2, 2, 32, 1536), BF16),
            pltpu.VMEM((2, 4, 32, 1536), BF16),
            pltpu.VMEM((3, 32, 1536), BF16),
            pltpu.VMEM((8, 48, 1536), BF16),
            pltpu.VMEM((8, 8, 48, 384), BF16),
            pltpu.VMEM((8, 48, 3072), BF16),
            pltpu.VMEM((2, 384, 768), BF16),
            pltpu.VMEM((12, 48, 128), F32),
            pltpu.VMEM((12, 48, 128), F32),
            pltpu.VMEM((12, 48, 128), F32),
            pltpu.VMEM((8, 48, 128), F32),
            pltpu.VMEM((8, 24, 128), F32),
            pltpu.VMEM((8, 24, 128), F32),
            pltpu.VMEM((8, 24, 128), F32),
            pltpu.VMEM((8, 24, 128), F32),
            pltpu.SemaphoreType.DMA((12,)),
            pltpu.SemaphoreType.DMA((N_COPY,)),
            pltpu.SemaphoreType.DMA((N_COPY,)),
        ],
        compiler_params=pltpu.CompilerParams(
            collective_id=0, has_side_effects=True, vmem_limit_bytes=60 * 1024 * 1024
        ),
    )(
        image_len,
        step_index,
        fresh_slots,
        fresh_pos,
        queries[0, 0],
        text_cache[0, 0],
        image_cache[0, 0],
        fresh_kv[0, 0].transpose(1, 0, 2),
        stream[0],
        modulation,
        out_weight.reshape(2, 48, 384),
        up_weight.reshape(2, 96, 1536),
        down_weight.T.reshape(2, 96, 1536),
        final_weight.T,
        latent[0],
    )
    return (both[0][None], both[1][None])


def solution(mesh):
    in_specs = (
        P("cfg", "req", "seq", None),
        P("cfg", "req", None, None, None),
        P("cfg", "req", None, None, None),
        P("cfg", "req", None, "seq", None),
        P("req", None),
        P(None, "req", "seq"),
        P(),
        P("cfg", None, "seq", "req"),
        P(),
        P("seq", "req"),
        P("seq", "req"),
        P("req", "seq"),
        P(),
        P("req", "seq", "cfg"),
        P(),
    )
    out_specs = (P("req", "seq", "cfg"), P("req", "seq", "cfg"))
    return jax.shard_map(
        per_device, mesh=mesh, in_specs=in_specs, out_specs=out_specs, check_vma=False
    )
```
